128 devices in a mesh: row: 8 (over z_lo, x), col: 16 (over y, z_hi, core).
Axes of the slice: x: 4, y: 4, z: 4 (z_hi: 2, z_lo: 2; z = z_hi * 2 + z_lo), core: 2. Of those that a mesh axis runs over, the one named last changes fastest.
Arguments:
- positions: float32 [3, 16384, 128], P(None, ('row', 'col')), may hold values from -6 to 6
- block_links: int32 [2, 16384], replicated, may hold values from 0 to 16383, as said below
- panel_points: int32 [8, 256], replicated, may hold values from 0 to 2097151
Outputs:
- smoothed: float32 [3, 32768, 128], P(None, ('row', 'col'))
- velocity: float32 [8, 3, 256], P('row', None, 'col')
The draws below stay inside these ranges and needn't reach their ends.
Inputs may be any that keep to these rules, and one draw needn't show every extreme that they name: block_links[0, b] is an owner device, numbered in the order of row+col; block_links[1] is a permutation of the 16384 blocks whose cycles are the loops, and all blocks of one loop have one owner. The 128 blocks of one device, b // 128, include at most 2 of any one owner, and in every draw one owner has exactly 2 blocks on every device.
All inputs are finite; a program needn't handle non-finite values.
Results may differ from the reference program's by a relative error of at most 0.0003.
Values sent between devices are 32-bit elements; how exact they have to be, the bound alone decides.
A program may use at most 128 MiB of HBM per device.

```python
import math
import jax
import jax.numpy as jnp
from jax import lax

BLK = 128
PANEL = 256
SWEEPS = 2
SLOT_DEV = 128
CAP = 2
NSTORE = 16384
NOWN = 32768
POINTS = 2097152
N_ROW = 8
DEVICES = 128


def loop_tables(key):
    key_busy, key_owner, key_order, key_break = jax.random.split(jax.random.fold_in(key, 11), 4)
    busiest = jax.random.randint(key_busy, (), 0, DEVICES, dtype=jnp.int32)
    others = jnp.arange(DEVICES - 1, dtype=jnp.int32)
    others = others + (others >= busiest).astype(jnp.int32)
    spares = jnp.repeat(others, CAP)

    def one_device(dev_key):
        key_remain, key_mix = jax.random.split(dev_key)
        remain = jax.random.permutation(key_remain, spares)[:SLOT_DEV - CAP]
        chosen = jnp.concatenate([jnp.full((CAP,), busiest, jnp.int32), remain])
        return jax.random.permutation(key_mix, chosen)
    owners = jax.vmap(one_device)(jax.random.split(key_owner, DEVICES)).reshape(NSTORE).astype(jnp.int32)
    shuffle = jax.random.permutation(key_order, NSTORE).astype(jnp.int32)
    orders = jnp.argsort(owners * NSTORE + shuffle).astype(jnp.int32)
    sorted_owner = owners[orders]
    indices = jnp.arange(NSTORE, dtype=jnp.int32)
    breaks = jax.random.randint(key_break, (NSTORE,), 0, 4) != 0
    change = jnp.concatenate([jnp.ones((1,), bool), sorted_owner[1:] != sorted_owner[:-1]])
    begins = jnp.logical_or(breaks, change)
    starts = lax.cummax(jnp.where(begins, indices, 0), axis=0)
    starts_at = jnp.where(begins, indices, NSTORE).astype(jnp.int32)
    following = lax.cummin(jnp.concatenate([starts_at[1:], jnp.full((1,), NSTORE, jnp.int32)]), axis=0, reverse=True)
    finish = following - 1
    step_to = jnp.where(indices < finish, indices + 1, starts)
    follows = jnp.zeros((NSTORE,), jnp.int32).at[orders].set(orders[step_to])
    return jnp.stack([owners, follows])


def draw_block_links(key, part):
    return loop_tables(key)


def with_ends(entries, key, least, top_value):
    place = [jax.random.randint(jax.random.fold_in(key, axis), (), 0, length) for axis, length in enumerate(entries.shape)]
    widest = entries.shape.index(max(entries.shape))
    neighbour = place[:widest] + [(place[widest] + 1) % entries.shape[widest]] + place[widest + 1:]
    return entries.at[tuple(place)].set(least).at[tuple(neighbour)].set(top_value)


def block_levels(rng, dims, shards, least, top_value):
    level = 1.0
    for dim, blocks in shards:
        draws = jax.random.uniform(jax.random.fold_in(jax.random.fold_in(rng, 6), dim), (blocks,), jnp.float32, least / len(shards), top_value / len(shards))
        level = level * jnp.repeat(jnp.exp(draws), dims[dim] // blocks).reshape((-1,) + (1,) * (len(dims) - 1 - dim))
    return level


def centred(rng, extent, deviation, bound, cuts=(), kind=jnp.bfloat16):
    factor_of = block_levels(rng, extent, cuts, -0.22, 0.18) if cuts else 1.0
    values = jax.random.normal(rng, extent, jnp.float32) * deviation * factor_of
    return jnp.minimum(jnp.maximum(values, -bound), bound).astype(kind)


def setup_inputs(seed: int = 0) -> dict:
    streams_of = jax.random.split(jax.random.key(seed), 4)
    return {
        "positions": centred(streams_of[0], (3, NSTORE, BLK), 1.0, 6.0, ((1, 128),), jnp.float32),
        "block_links": draw_block_links(jax.random.fold_in(streams_of[3], 71), 0),
        "panel_points": with_ends(jax.random.randint(streams_of[2], (N_ROW, PANEL), 0, POINTS), jax.random.fold_in(streams_of[2], 1), 0, POINTS - 1).astype(jnp.int32),
    }


SMOOTH_RATE = 0.25
CORE_SQUARED = 0.01

def cross_three(left_vec, right_vec):
    return jnp.stack([left_vec[1] * right_vec[2] - left_vec[2] * right_vec[1], left_vec[2] * right_vec[0] - left_vec[0] * right_vec[2], left_vec[0] * right_vec[1] - left_vec[1] * right_vec[0]])

def neighbours(points, next_block, prev_block):
    ahead = jnp.concatenate([points[:, :, 1:], points[:, next_block, :1]], axis=2)
    behind = jnp.concatenate([points[:, prev_block, -1:], points[:, :, :-1]], axis=2)
    return (behind, ahead)

def smooth_loops(points, next_block, prev_block):
    for sweep_no in range(SWEEPS):
        behind, ahead = neighbours(points, next_block, prev_block)
        points = points + SMOOTH_RATE * (behind - 2.0 * points + ahead)
    return points

def panel_sums(targets, sources):
    centres = sources[:3]
    segments = sources[3:]
    inner = lax.dot_general(targets, centres, (((0,), (0,)), ((), ())), precision=lax.Precision.HIGHEST)
    squared = lax.optimization_barrier(jnp.sum(targets * targets, 0))[:, None] + lax.optimization_barrier(jnp.sum(centres * centres, 0))[None, :] - 2.0 * inner + CORE_SQUARED
    weights = 1.0 / (squared * jnp.sqrt(squared))
    features = jnp.concatenate([segments, cross_three(segments, centres)], 0)
    return lax.dot_general(weights, features, (((1,), (1,)), ((), ())), precision=lax.Precision.HIGHEST)

def reference(positions, block_links, panel_points):
    owners = block_links[0]
    follows = block_links[1]
    counter = jnp.arange(NSTORE, dtype=jnp.int32)
    precedes = jnp.zeros_like(follows).at[follows].set(counter)
    smoothed = smooth_loops(positions, follows, precedes)
    owner_grid = owners.reshape(DEVICES, SLOT_DEV)
    same_owner = owner_grid[:, :, None] == owner_grid[:, None, :]
    earlier = jnp.arange(SLOT_DEV)[None, :] < jnp.arange(SLOT_DEV)[:, None]
    ranks = lax.optimization_barrier(jnp.sum(jnp.logical_and(same_owner, earlier[None]), axis=2)).astype(jnp.int32).reshape(NSTORE)
    places = owners * (DEVICES * CAP) + counter // SLOT_DEV * CAP + ranks
    layout = jnp.zeros((3, NOWN, BLK), jnp.float32).at[:, places, :].set(smoothed)
    behind, ahead = neighbours(smoothed, follows, precedes)
    segments = ahead - smoothed
    centres = 0.5 * (ahead + smoothed)
    wanted = panel_points.reshape(-1)
    targets = smoothed[:, wanted // BLK, wanted % BLK]
    tiles = NSTORE // 128
    sources = jnp.concatenate([centres, segments], 0).reshape(6, tiles, 128 * BLK)
    sources = jnp.moveaxis(sources, 1, 0)

    def add_tile(running, tile):
        return (running + panel_sums(targets, tile), None)
    sums, unused = lax.scan(add_tile, jnp.zeros((wanted.shape[0], 6), jnp.float32), sources)
    scale = 1.0 / (math.pi * math.sqrt(NSTORE * BLK))
    velocity = scale * (cross_three(sums[:, :3].T, targets) - sums[:, 3:].T)
    velocity = jnp.transpose(velocity.reshape(3, N_ROW, PANEL), (1, 0, 2))
    return (layout, velocity)
```

```python
import functools
import math

import jax
import jax.numpy as jnp
from jax import lax
from jax.experimental import pallas as pl
from jax.experimental.pallas import tpu as pltpu
from jax.sharding import PartitionSpec as P

CORE_SQUARED = 0.01
F32 = jnp.float32
BF16 = jnp.bfloat16
LANES = 128
VMEM_LIMIT = 56 << 20
MESH = pl.DeviceIdType.MESH
CHUNK = 6
EDGE_LANES = (125, 126, 127, 0, 1)


def iota(shape, axis):
    return lax.broadcasted_iota(jnp.int32, shape, axis)


def three_parts(value):
    high = value.astype(BF16)
    rest = value - high.astype(F32)
    middle = rest.astype(BF16)
    return high, middle, (rest - middle.astype(F32)).astype(BF16)


def two_parts(value):
    high = value.astype(BF16)
    return high, (value - high.astype(F32)).astype(BF16)


def to_column(row, eye):
    return jnp.sum(jnp.where(eye, row, 0.0), axis=1, keepdims=True)


def to_row(column, eye):
    return jnp.sum(jnp.where(eye, column, 0.0), axis=0, keepdims=True)


def pick_rows(chooser, arrays):
    width = arrays[0].shape[1]
    parts = jnp.concatenate([part for array in arrays for part in three_parts(array)], axis=1)
    got = jnp.dot(chooser, parts, preferred_element_type=F32)
    result = []
    for n in range(len(arrays)):
        at = 3 * n * width
        result.append(
            got[:, at : at + width]
            + got[:, at + width : at + 2 * width]
            + got[:, at + 2 * width : at + 3 * width]
        )
    return result


def roll(value, shift):
    return pltpu.roll(value, shift % LANES, 1)


def prep_kernel(me_ref, pos_ref, links_ref, panel_ref, out_ref, tgt_ref):
    slots = pos_ref.shape[1]
    me = me_ref[0]
    base = me * slots
    eye = iota((slots, LANES), 0) == iota((slots, LANES), 1)
    here = pl.ds(pl.multiple_of(base, LANES), LANES)
    owner_row = links_ref[0:1, here].astype(F32)
    follow_row = links_ref[1:2, here].astype(F32)
    owner_col = to_column(owner_row, eye)
    follow_col = to_column(follow_row, eye)
    earlier = iota((slots, LANES), 0) < iota((slots, LANES), 1)
    same = jnp.logical_and(owner_col == owner_row, earlier)
    rank_row = jnp.sum(jnp.where(same, 1.0, 0.0), axis=0, keepdims=True)
    slot_row = owner_row * 2.0 + rank_row
    held = out_ref.shape[1]
    chooser = (iota((held, LANES), 0).astype(F32) == slot_row).astype(BF16)
    raw = [pos_ref[c] for c in range(3)]
    for c, moved in enumerate(pick_rows(chooser, raw)):
        out_ref[c] = moved

    mine_col = (base + iota((slots, 1), 0)).astype(F32)
    blocks = links_ref.shape[1]
    lane_row = iota((1, LANES), 1).astype(F32)

    def look(turn, total):
        at = pl.multiple_of(turn * LANES, LANES)
        row = links_ref[1:2, pl.ds(at, LANES)].astype(F32)
        number = lane_row + (turn * LANES).astype(F32)
        return total + jnp.where(row == mine_col, number, 0.0)

    precede_col = jnp.sum(
        lax.fori_loop(0, blocks // LANES, look, jnp.zeros((slots, LANES), F32), unroll=8),
        axis=1,
        keepdims=True,
    )

    lane = iota((slots, LANES), 1)
    rows = []
    for c in range(3):
        x = raw[c]
        b1, b2, a1, a2 = roll(x, 1), roll(x, 2), roll(x, -1), roll(x, -2)
        zero = jnp.zeros_like(x)
        wrap = (
            4.0 * (jnp.where(lane < 1, b1, zero) + jnp.where(lane > LANES - 2, a1, zero))
            + (jnp.where(lane < 2, b2, zero) + jnp.where(lane > LANES - 3, a2, zero))
        )
        inside = (
            6.0 * x
            + 4.0 * (jnp.where(lane < 1, zero, b1) + jnp.where(lane > LANES - 2, zero, a1))
            + (jnp.where(lane < 2, zero, b2) + jnp.where(lane > LANES - 3, zero, a2))
        )
        rows += [inside * 0.0625, wrap * 0.0625]
    stack = jnp.concatenate(rows, axis=0)
    parts = jnp.concatenate(three_parts(stack), axis=0)
    high = stack.shape[0]
    width = panel_ref.shape[1]
    per_half = tgt_ref.shape[1] // width
    tgt_ref[...] = jnp.zeros_like(tgt_ref)
    for r in range(panel_ref.shape[0]):
        flat = panel_ref[r : r + 1, :]
        block = (flat // LANES).astype(F32)
        point = flat % LANES
        one_point = (iota((LANES, width), 0) == point).astype(BF16)
        got = jnp.dot(parts, one_point, preferred_element_type=F32)
        got = got[:high] + got[high : 2 * high] + got[2 * high :]
        here_mask = block == mine_col
        edge_mask = jnp.logical_or(
            jnp.logical_and(precede_col == block, point >= LANES - 2),
            jnp.logical_and(follow_col == block, point <= 1),
        )
        for c in range(3):
            at = 2 * c * slots
            value = jnp.where(here_mask, got[at : at + slots], 0.0) + jnp.where(
                edge_mask, got[at + slots : at + 2 * slots], 0.0
            )
            row = (r // per_half) * 3 + c
            col = (r % per_half) * width
            tgt_ref[row : row + 1, col : col + width] = jnp.sum(value, axis=0, keepdims=True)


def exchange_kernel(
    n_row, n_col, out_ref, part_ref, arrived_ref, tgt_ref,
    row_in, total, col_in, send_sem, recv_sem, own_sem,
    s1, r1, s2, r2, s3, r3,
):
    me_r = lax.axis_index("row")
    me_c = lax.axis_index("col")
    me = me_r * n_col + me_c
    n = n_row * n_col
    width = total.shape[1]

    def slice_of(ref, r):
        return ref.at[:, pl.ds(pl.multiple_of(r * width, width), width)]

    first = []
    for step in range(1, n_row):
        to = lax.rem(me_r + step, n_row)
        copy = pltpu.make_async_remote_copy(
            src_ref=slice_of(part_ref, to),
            dst_ref=row_in.at[me_r],
            send_sem=s1.at[step],
            recv_sem=r1.at[me_r],
            device_id=(to, me_c),
            device_id_type=MESH,
        )
        copy.start()
        first.append(copy)

    def start_block(step, carry):
        to = lax.rem(me + step, n)
        pltpu.make_async_remote_copy(
            src_ref=out_ref.at[:, to],
            dst_ref=arrived_ref.at[:, me],
            send_sem=send_sem,
            recv_sem=recv_sem,
            device_id=(to // n_col, lax.rem(to, n_col)),
            device_id_type=MESH,
        ).start()
        return carry

    lax.fori_loop(1, n, start_block, 0)
    own = pltpu.make_async_copy(out_ref.at[:, me], arrived_ref.at[:, me], own_sem)
    own.start()

    row_in[me_r] = part_ref[:, pl.ds(pl.multiple_of(me_r * width, width), width)]
    for step in range(1, n_row):
        frm = lax.rem(me_r + step, n_row)
        pltpu.make_async_copy(row_in.at[frm], row_in.at[frm], r1.at[frm]).wait()
    value = row_in[0]
    for r in range(1, n_row):
        value = value + row_in[r]
    total[...] = value
    second = []
    for step in range(1, n_col):
        to = lax.rem(me_c + step, n_col)
        copy = pltpu.make_async_remote_copy(
            src_ref=total,
            dst_ref=col_in.at[me_c],
            send_sem=s2.at[step],
            recv_sem=r2.at[me_c],
            device_id=(me_r, to),
            device_id_type=MESH,
        )
        copy.start()
        second.append(copy)
    col_in[me_c] = value
    for step in range(1, n_col):
        frm = lax.rem(me_c + step, n_col)
        pltpu.make_async_copy(col_in.at[frm], col_in.at[frm], r2.at[frm]).wait()
    value = col_in[0]
    for c in range(1, n_col):
        value = value + col_in[c]
    tgt_ref[:, pl.ds(pl.multiple_of(me_r * width, width), width)] = value
    third = []
    for step in range(1, n_row):
        to = lax.rem(me_r + step, n_row)
        copy = pltpu.make_async_remote_copy(
            src_ref=slice_of(tgt_ref, me_r),
            dst_ref=slice_of(tgt_ref, me_r),
            send_sem=s3.at[step],
            recv_sem=r3.at[me_r],
            device_id=(to, me_c),
            device_id_type=MESH,
        )
        copy.start()
        third.append(copy)
    for step in range(1, n_row):
        frm = lax.rem(me_r + step, n_row)
        pltpu.make_async_copy(slice_of(tgt_ref, frm), slice_of(tgt_ref, frm), r3.at[frm]).wait()
    for copy in first + second + third:
        copy.wait_send()
    rest = pl.ds(0, n - 1)
    pltpu.make_async_copy(out_ref.at[:, rest], out_ref.at[:, rest], send_sem).wait()
    pltpu.make_async_copy(arrived_ref.at[:, rest], arrived_ref.at[:, rest], recv_sem).wait()
    own.wait()


def features(centres, segments):
    rows = []
    for c in centres:
        high, middle, low = (part.astype(F32) for part in three_parts(c))
        rows += [high, middle, high, low, high, middle]
    square = centres[0] * centres[0] + centres[1] * centres[1] + centres[2] * centres[2]
    rows += [part.astype(F32) for part in three_parts(square)]
    rows += [jnp.ones_like(square)] * 3
    s, c = segments, centres
    six = [s[0], s[1], s[2]]
    six += [s[1] * c[2] - s[2] * c[1], s[2] * c[0] - s[0] * c[2], s[0] * c[1] - s[1] * c[0]]
    pairs = [two_parts(value) for value in six]
    return rows, [pair[0].astype(F32) for pair in pairs], [pair[1].astype(F32) for pair in pairs]


def velocity_kernel(
    scale, me_ref, pos_ref, arrived_ref, grid_ref, tgt_ref, smooth_ref, vel_ref,
    b_ref, f_ref, a_ref, acc_ref,
):
    slots = pos_ref.shape[1]
    held = arrived_ref.shape[1]
    me = me_ref[0].astype(F32)
    b_ref[...] = jnp.zeros_like(b_ref)
    f_ref[...] = jnp.zeros_like(f_ref)
    a_ref[...] = jnp.zeros_like(a_ref)

    half = tgt_ref.shape[1]
    for h in range(2):
        at = slice(h * half, (h + 1) * half)
        t = [tgt_ref[h * 3 + c : h * 3 + c + 1, :] for c in range(3)]
        rows = []
        for value in t:
            high, middle, low = (part.astype(F32) for part in three_parts(-2.0 * value))
            rows += [high, high, middle, high, low, middle]
        rows += [jnp.ones_like(t[0])] * 3
        square = t[0] * t[0] + t[1] * t[1] + t[2] * t[2] + CORE_SQUARED
        rows += [part.astype(F32) for part in three_parts(square)]
        for k, row in enumerate(rows):
            a_ref[k : k + 1, at] = row

    lane = iota((slots, LANES), 1)
    inner = jnp.logical_and(lane >= 2, lane < LANES - 3)
    centres, segments = [], []
    for c in range(3):
        x = pos_ref[c]
        sm = (6.0 * x + 4.0 * (roll(x, 1) + roll(x, -1)) + (roll(x, 2) + roll(x, -2))) * 0.0625
        ahead = roll(sm, -1)
        segments.append(jnp.where(inner, ahead - sm, 0.0))
        centres.append(0.5 * (ahead + sm))
    rows, highs, lows = features(centres, segments)
    for k, row in enumerate(rows):
        b_ref[pl.ds(k, slots, stride=32), :] = row
    for k in range(6):
        f_ref[pl.ds(k, slots, stride=16), :] = highs[k]
        f_ref[pl.ds(8 + k, slots, stride=16), :] = lows[k]

    n = grid_ref.shape[1]
    owners = grid_ref[0].astype(F32)
    follows = grid_ref[1].astype(F32)
    square_eye = iota((n, LANES), 0) == iota((n, LANES), 1)
    number = (iota((n, LANES), 0) * LANES + iota((n, LANES), 1)).astype(F32)
    mine = owners == me
    before = (iota((LANES, LANES), 0) < iota((LANES, LANES), 1)).astype(BF16)
    rank = jnp.dot(mine.astype(BF16), before, preferred_element_type=F32)
    id_col = jnp.zeros((held, 1), F32)
    next_col = jnp.zeros((held, 1), F32)
    for k in range(2):
        chosen = jnp.logical_and(mine, rank == float(k))
        count = jnp.sum(jnp.where(chosen, 1.0, 0.0), axis=1, keepdims=True)
        ids = jnp.sum(jnp.where(chosen, number, 0.0), axis=1, keepdims=True)
        nexts = jnp.sum(jnp.where(chosen, follows, 0.0), axis=1, keepdims=True)
        ids = jnp.where(count > 0.5, ids, -1.0)
        nexts = jnp.where(count > 0.5, nexts, -2.0)
        place = iota((held, LANES), 0) == 2 * iota((held, LANES), 1) + k
        id_col = id_col + to_column(to_row(ids, square_eye), place)
        next_col = next_col + to_column(to_row(nexts, square_eye), place)
    held_eye = iota((held, held), 0) == iota((held, held), 1)
    id_row = to_row(id_col, held_eye)
    next_row = to_row(next_col, held_eye)
    y = [arrived_ref[c] for c in range(3)]
    nxt = pick_rows((next_col == id_row).astype(BF16), y)
    prv = pick_rows((id_col == next_row).astype(BF16), y)
    lane = iota((held, LANES), 1)
    arrays = []
    for c in range(3):
        v, nx, pv = y[c], nxt[c], prv[c]
        a1 = jnp.where(lane < LANES - 1, roll(v, -1), roll(nx, -1))
        a2 = jnp.where(lane < LANES - 2, roll(v, -2), roll(nx, -2))
        b1 = jnp.where(lane < 1, roll(pv, 1), roll(v, 1))
        b2 = jnp.where(lane < 2, roll(pv, 2), roll(v, 2))
        sm = (6.0 * v + 4.0 * (a1 + b1) + (a2 + b2)) * 0.0625
        smooth_ref[c] = sm
        after = (
            6.0 * roll(nx, -1) + 4.0 * (roll(nx, -2) + v) + (roll(nx, -3) + roll(v, 1))
        ) * 0.0625
        ahead = jnp.where(lane < LANES - 1, roll(sm, -1), after)
        arrays += [0.5 * (ahead + sm), ahead - sm]
    pick = jnp.zeros((8, LANES), jnp.bool_)
    for j, where in enumerate(EDGE_LANES):
        pick = jnp.logical_or(
            pick, jnp.logical_and(iota((8, LANES), 0) == j, iota((8, LANES), 1) == where)
        )
    stack = jnp.concatenate([part for array in arrays for part in three_parts(array)], axis=0)
    got = lax.dot_general(
        pick.astype(BF16), stack, (((1,), (1,)), ((), ())), preferred_element_type=F32
    )
    got = [
        got[:, 3 * m * held : (3 * m + 1) * held]
        + got[:, (3 * m + 1) * held : (3 * m + 2) * held]
        + got[:, (3 * m + 2) * held : (3 * m + 3) * held]
        for m in range(6)
    ]
    rows, highs, lows = features(got[0::2], got[1::2])
    for h in range(held // LANES):
        at = slice(h * LANES, (h + 1) * LANES)
        step = held // LANES
        for k, row in enumerate(rows):
            b_ref[pl.ds((slots + h) * 32 + k, 8, stride=32 * step), :] = row[:, at]
        for k in range(6):
            f_ref[pl.ds((slots + h) * 16 + k, 8, stride=16 * step), :] = highs[k][:, at]
            f_ref[pl.ds((slots + h) * 16 + 8 + k, 8, stride=16 * step), :] = lows[k][:, at]

    acc_ref[...] = jnp.zeros_like(acc_ref)
    used = slots + len(EDGE_LANES) * (held // LANES)
    a = a_ref[...].astype(BF16)

    def chunk(turn, carry):
        b_at = pl.multiple_of(turn * (CHUNK * 32), 32)
        f_at = pl.multiple_of(turn * (CHUNK * 16), 16)
        b = jnp.concatenate(
            [b_ref[pl.ds(b_at + 32 * j, 32), :].astype(BF16) for j in range(CHUNK)], axis=1
        )
        f = jnp.concatenate(
            [f_ref[pl.ds(f_at + 16 * j, 16), :].astype(BF16) for j in range(CHUNK)], axis=1
        )
        q = lax.dot_general(b, a, (((0,), (0,)), ((), ())), preferred_element_type=F32)
        r = lax.rsqrt(q)
        high, low = two_parts(r * r * r)
        acc_ref[...] += jnp.dot(f, high, preferred_element_type=F32) + jnp.dot(
            f, low, preferred_element_type=F32
        )
        return carry

    lax.fori_loop(0, used // CHUNK, chunk, 0)
    vel_ref[...] = jnp.zeros_like(vel_ref)
    for h in range(2):
        at = slice(h * half, (h + 1) * half)
        t = [tgt_ref[h * 3 + c : h * 3 + c + 1, :] for c in range(3)]
        s = [acc_ref[k : k + 1, at] + acc_ref[8 + k : 9 + k, at] for k in range(6)]
        vel_ref[0:1, at] = scale * (s[1] * t[2] - s[2] * t[1] - s[3])
        vel_ref[1:2, at] = scale * (s[2] * t[0] - s[0] * t[2] - s[4])
        vel_ref[2:3, at] = scale * (s[0] * t[1] - s[1] * t[0] - s[5])


def reduce_kernel(n_row, n_col, part_ref, out_ref, row_in, total, col_in, s1, r1, s2, r2):
    me_r = lax.axis_index("row")
    me_c = lax.axis_index("col")
    width = total.shape[1]
    first = []
    for step in range(1, n_row):
        to = lax.rem(me_r + step, n_row)
        copy = pltpu.make_async_remote_copy(
            src_ref=part_ref.at[:, pl.ds(pl.multiple_of(to * width, width), width)],
            dst_ref=row_in.at[me_r],
            send_sem=s1.at[step],
            recv_sem=r1.at[me_r],
            device_id=(to, me_c),
            device_id_type=MESH,
        )
        copy.start()
        first.append(copy)
    row_in[me_r] = part_ref[:, pl.ds(pl.multiple_of(me_r * width, width), width)]
    for step in range(1, n_row):
        frm = lax.rem(me_r + step, n_row)
        pltpu.make_async_copy(row_in.at[frm], row_in.at[frm], r1.at[frm]).wait()
    value = row_in[0]
    for r in range(1, n_row):
        value = value + row_in[r]
    total[...] = value
    second = []
    for step in range(1, n_col):
        to = lax.rem(me_c + step, n_col)
        copy = pltpu.make_async_remote_copy(
            src_ref=total,
            dst_ref=col_in.at[me_c],
            send_sem=s2.at[step],
            recv_sem=r2.at[me_c],
            device_id=(me_r, to),
            device_id_type=MESH,
        )
        copy.start()
        second.append(copy)
    col_in[me_c] = value
    for step in range(1, n_col):
        frm = lax.rem(me_c + step, n_col)
        pltpu.make_async_copy(col_in.at[frm], col_in.at[frm], r2.at[frm]).wait()
    value = col_in[0]
    for c in range(1, n_col):
        value = value + col_in[c]
    out_ref[...] = value
    for copy in first + second:
        copy.wait_send()


def shards(n_row, n_col, positions, block_links, panel_points):
    devices = n_row * n_col
    slots, block_len = positions.shape[1:]
    held = 2 * slots
    blocks = block_links.shape[1]
    groups, panel = panel_points.shape
    targets = groups * panel
    vmem = pl.BlockSpec(memory_space=pltpu.VMEM)
    smem = pl.BlockSpec(memory_space=pltpu.SMEM)
    hbm = pl.BlockSpec(memory_space=pl.ANY)
    params = pltpu.CompilerParams(vmem_limit_bytes=VMEM_LIMIT)
    remote = pltpu.CompilerParams(has_side_effects=True)
    me = lax.axis_index(("row", "col")).astype(jnp.int32).reshape(1)
    outgoing, partial_targets = pl.pallas_call(
        prep_kernel,
        out_shape=(
            jax.ShapeDtypeStruct((3, held, block_len), F32),
            jax.ShapeDtypeStruct((8, targets // 2), F32),
        ),
        in_specs=[smem, vmem, vmem, vmem],
        out_specs=(vmem, vmem),
        compiler_params=params,
        name="prep",
    )(me, positions, block_links, panel_points)
    width = targets // 2 // n_row
    dma = pltpu.SemaphoreType.DMA
    arrived, all_targets = pl.pallas_call(
        functools.partial(exchange_kernel, n_row, n_col),
        out_shape=(
            jax.ShapeDtypeStruct((3, devices, 2, block_len), F32),
            jax.ShapeDtypeStruct((8, targets // 2), F32),
        ),
        in_specs=[hbm, vmem],
        out_specs=(hbm, vmem),
        scratch_shapes=[
            pltpu.VMEM((n_row, 8, width), F32),
            pltpu.VMEM((8, width), F32),
            pltpu.VMEM((n_col, 8, width), F32),
            dma, dma, dma,
            dma((n_row,)), dma((n_row,)),
            dma((n_col,)), dma((n_col,)),
            dma((n_row,)), dma((n_row,)),
        ],
        compiler_params=remote,
        name="exchange",
    )(outgoing.reshape(3, devices, 2, block_len), partial_targets)
    stored = -(-(slots + 8 * (held // LANES)) // CHUNK) * CHUNK
    scale = 1.0 / (math.pi * math.sqrt(blocks * block_len))
    smoothed, partial_velocity = pl.pallas_call(
        functools.partial(velocity_kernel, scale),
        out_shape=(
            jax.ShapeDtypeStruct((3, held, block_len), F32),
            jax.ShapeDtypeStruct((8, targets), F32),
        ),
        in_specs=[smem, vmem, vmem, vmem, vmem],
        out_specs=(vmem, vmem),
        scratch_shapes=[
            pltpu.VMEM((stored * 32, LANES), F32),
            pltpu.VMEM((stored * 16, LANES), F32),
            pltpu.VMEM((32, targets), F32),
            pltpu.VMEM((16, targets), F32),
        ],
        compiler_params=params,
        name="velocity",
    )(
        me,
        positions,
        arrived.reshape(3, held, block_len),
        block_links.reshape(2, devices, slots),
        all_targets,
    )
    summed = pl.pallas_call(
        functools.partial(reduce_kernel, n_row, n_col),
        out_shape=jax.ShapeDtypeStruct((8, panel), F32),
        in_specs=[vmem],
        out_specs=vmem,
        scratch_shapes=[
            pltpu.VMEM((n_row, 8, panel), F32),
            pltpu.VMEM((8, panel), F32),
            pltpu.VMEM((n_col, 8, panel), F32),
            dma((n_row,)), dma((n_row,)),
            dma((n_col,)), dma((n_col,)),
        ],
        compiler_params=remote,
        name="reduce",
    )(partial_velocity)
    share = panel // n_col
    part = lax.dynamic_slice(summed, (0, lax.axis_index("col") * share), (3, share))
    return smoothed, part[None]


def solution(mesh):
    placed = (P(None, ("row", "col"), None), P(), P())
    return jax.shard_map(
        functools.partial(shards, mesh.shape["row"], mesh.shape["col"]),
        mesh=mesh,
        in_specs=placed,
        out_specs=(P(None, ("row", "col"), None), P("row", None, "col")),
        check_vma=False,
    )
```

```python
import functools
import math

import jax
import jax.numpy as jnp
from jax import lax
from jax.experimental import pallas as pl
from jax.experimental.pallas import tpu as pltpu
from jax.sharding import PartitionSpec as P

CORE_SQUARED = 0.01
F32 = jnp.float32
BF16 = jnp.bfloat16
LANES = 128
VMEM_LIMIT = 56 << 20
MESH = pl.DeviceIdType.MESH
CHUNK = 8
EDGE_LANES = (125, 126, 127, 0, 1)


def iota(shape, axis):
    return lax.broadcasted_iota(jnp.int32, shape, axis)


def three_parts(value):
    high = value.astype(BF16)
    rest = value - high.astype(F32)
    middle = rest.astype(BF16)
    return high, middle, (rest - middle.astype(F32)).astype(BF16)


def two_parts(value):
    high = value.astype(BF16)
    return high, (value - high.astype(F32)).astype(BF16)


def to_column(row, eye):
    return jnp.sum(jnp.where(eye, row, 0.0), axis=1, keepdims=True)


def to_row(column, eye):
    return jnp.sum(jnp.where(eye, column, 0.0), axis=0, keepdims=True)


def pick_rows(chooser, arrays):
    width = arrays[0].shape[1]
    parts = jnp.concatenate([part for array in arrays for part in three_parts(array)], axis=1)
    got = jnp.dot(chooser, parts, preferred_element_type=F32)
    result = []
    for n in range(len(arrays)):
        at = 3 * n * width
        result.append(
            got[:, at : at + width]
            + got[:, at + width : at + 2 * width]
            + got[:, at + 2 * width : at + 3 * width]
        )
    return result


def roll(value, shift):
    return pltpu.roll(value, shift % LANES, 1)


def features(centres, segments):
    rows = []
    for c in centres:
        high, middle, low = (part.astype(F32) for part in three_parts(c))
        rows += [high, middle, high, low, high, middle]
    square = centres[0] * centres[0] + centres[1] * centres[1] + centres[2] * centres[2]
    rows += [part.astype(F32) for part in three_parts(square)]
    rows += [jnp.ones_like(square)] * 3
    s, c = segments, centres
    six = [s[0], s[1], s[2]]
    six += [s[1] * c[2] - s[2] * c[1], s[2] * c[0] - s[0] * c[2], s[0] * c[1] - s[1] * c[0]]
    pairs = [two_parts(value) for value in six]
    return rows, [pair[0].astype(F32) for pair in pairs], [pair[1].astype(F32) for pair in pairs]


def step_kernel(
    n_row, n_col, scale, pos_ref, links_ref, panel_ref, smooth_ref, vel_ref,
    grid_ref, part_ref, tgt_ref, send_ref, arrived_ref, b_ref, f_ref, a_ref, acc_ref,
    pair_ref, sum_ref, row_in, total, col_in, row_sum, row_total, col_sum,
    send_sem, recv_sem, s1, r1, s2, r2, s3, r3, s4, r4, s5, r5,
):
    me_r = lax.axis_index("row")
    me_c = lax.axis_index("col")
    me = me_r * n_col + me_c
    n = n_row * n_col
    slots = pos_ref.shape[1]
    held = 2 * n

    barrier = pltpu.get_barrier_semaphore()
    for step in range(1, n_row):
        to = lax.rem(me_r + step, n_row)
        pl.semaphore_signal(barrier, inc=1, device_id=(to, me_c), device_id_type=MESH)
    for step in range(1, n_col):
        to = lax.rem(me_c + step, n_col)
        pl.semaphore_signal(barrier, inc=1, device_id=(me_r, to), device_id_type=MESH)

    def send_row(source, target, send, recv):
        copies = []
        for step in range(1, n_row):
            to = lax.rem(me_r + step, n_row)
            copy = pltpu.make_async_remote_copy(
                src_ref=source(to),
                dst_ref=target(me_r),
                send_sem=send.at[step],
                recv_sem=recv.at[me_r],
                device_id=(to, me_c),
                device_id_type=MESH,
            )
            copy.start()
            copies.append(copy)
        return copies

    def send_col(source, target, send, recv):
        copies = []
        for step in range(1, n_col):
            to = lax.rem(me_c + step, n_col)
            copy = pltpu.make_async_remote_copy(
                src_ref=source,
                dst_ref=target(me_c),
                send_sem=send.at[step],
                recv_sem=recv.at[me_c],
                device_id=(me_r, to),
                device_id_type=MESH,
            )
            copy.start()
            copies.append(copy)
        return copies

    def wait_from(mine, count, target, recv):
        for step in range(1, count):
            frm = lax.rem(mine + step, count)
            pltpu.make_async_copy(target(frm), target(frm), recv.at[frm]).wait()

    def add_up(ref, count):
        value = ref[0]
        for r in range(1, count):
            value = value + ref[r]
        return value

    eye = iota((slots, LANES), 0) == iota((slots, LANES), 1)
    here = pl.ds(pl.multiple_of(me * slots, LANES), LANES)
    owner_row = links_ref[0:1, here].astype(F32)
    follow_row = links_ref[1:2, here].astype(F32)
    follow_col = to_column(follow_row, eye)
    mine_col = (me * slots + iota((slots, 1), 0)).astype(F32)
    lane_row = iota((1, LANES), 1).astype(F32)

    def look(turn, found):
        at = pl.multiple_of(turn * LANES, LANES)
        row = links_ref[1:2, pl.ds(at, LANES)].astype(F32)
        grid_ref[1, pl.ds(turn, 1), :] = row
        grid_ref[0, pl.ds(turn, 1), :] = links_ref[0:1, pl.ds(at, LANES)].astype(F32)
        number = lane_row + (turn * LANES).astype(F32)
        return found + jnp.where(row == mine_col, number, 0.0)

    precede_col = jnp.sum(
        lax.fori_loop(0, n, look, jnp.zeros((slots, LANES), F32), unroll=8),
        axis=1,
        keepdims=True,
    )
    raw = [pos_ref[c] for c in range(3)]
    lane = iota((slots, LANES), 1)
    rows = []
    for x in raw:
        b1, b2, a1, a2 = roll(x, 1), roll(x, 2), roll(x, -1), roll(x, -2)
        zero = jnp.zeros_like(x)
        wrap = (
            4.0 * (jnp.where(lane < 1, b1, zero) + jnp.where(lane > LANES - 2, a1, zero))
            + (jnp.where(lane < 2, b2, zero) + jnp.where(lane > LANES - 3, a2, zero))
        )
        inside = (
            6.0 * x
            + 4.0 * (jnp.where(lane < 1, zero, b1) + jnp.where(lane > LANES - 2, zero, a1))
            + (jnp.where(lane < 2, zero, b2) + jnp.where(lane > LANES - 3, zero, a2))
        )
        rows += [inside * 0.0625, wrap * 0.0625]
    stack = jnp.concatenate(rows, axis=0)
    parts = jnp.concatenate(three_parts(stack), axis=0)
    high = stack.shape[0]
    panel = panel_ref.shape[1]
    half = tgt_ref.shape[1]
    per_half = half // panel
    part_ref[...] = jnp.zeros_like(part_ref)
    for r in range(panel_ref.shape[0]):
        flat = panel_ref[r : r + 1, :]
        block = (flat // LANES).astype(F32)
        point = flat % LANES
        one_point = (iota((LANES, panel), 0) == point).astype(BF16)
        got = jnp.dot(parts, one_point, preferred_element_type=F32)
        got = got[:high] + got[high : 2 * high] + got[2 * high :]
        here_mask = block == mine_col
        edge_mask = jnp.logical_or(
            jnp.logical_and(precede_col == block, point >= LANES - 2),
            jnp.logical_and(follow_col == block, point <= 1),
        )
        for c in range(3):
            at = 2 * c * slots
            value = jnp.where(here_mask, got[at : at + slots], 0.0) + jnp.where(
                edge_mask, got[at + slots : at + 2 * slots], 0.0
            )
            row = (r // per_half) * 3 + c
            col = (r % per_half) * panel
            part_ref[row : row + 1, col : col + panel] = jnp.sum(value, axis=0, keepdims=True)

    width = half // n_row

    def piece(ref, r, size):
        return ref.at[:, pl.ds(pl.multiple_of(r * size, size), size)]

    pl.semaphore_wait(barrier, n_row + n_col - 2)
    copies = send_row(lambda to: piece(part_ref, to, width), lambda r: row_in.at[r], s1, r1)
    row_in[me_r] = part_ref[:, pl.ds(pl.multiple_of(me_r * width, width), width)]

    owner_col = to_column(owner_row, eye)
    earlier = iota((slots, LANES), 0) < iota((slots, LANES), 1)
    same = jnp.logical_and(owner_col == owner_row, earlier)
    rank_row = jnp.sum(jnp.where(same, 1.0, 0.0), axis=0, keepdims=True)
    send_ref[...] = jnp.zeros_like(send_ref)
    to_owner = iota((n, LANES), 0).astype(F32) == owner_row
    for k in range(2):
        chooser = jnp.logical_and(to_owner, rank_row == float(k)).astype(BF16)
        for c, moved in enumerate(pick_rows(chooser, raw)):
            send_ref[pl.ds(2 * c + k, n, stride=8), :] = moved

    wait_from(me_r, n_row, lambda r: row_in.at[r], r1)
    value = add_up(row_in, n_row)
    total[...] = value
    copies += send_col(total, lambda c: col_in.at[c], s2, r2)
    col_in[me_c] = value

    b_ref[...] = jnp.zeros_like(b_ref)
    f_ref[...] = jnp.zeros_like(f_ref)
    inner = jnp.logical_and(lane >= 2, lane < LANES - 3)
    centres, segments = [], []
    for x in raw:
        sm = (6.0 * x + 4.0 * (roll(x, 1) + roll(x, -1)) + (roll(x, 2) + roll(x, -2))) * 0.0625
        ahead = roll(sm, -1)
        segments.append(jnp.where(inner, ahead - sm, 0.0))
        centres.append(0.5 * (ahead + sm))
    rows, highs, lows = features(centres, segments)
    for k, row in enumerate(rows):
        b_ref[pl.ds(k, slots, stride=32), :] = row
    for k in range(6):
        f_ref[pl.ds(k, slots, stride=16), :] = highs[k]
        f_ref[pl.ds(8 + k, slots, stride=16), :] = lows[k]

    wait_from(me_c, n_col, lambda c: col_in.at[c], r2)
    value = add_up(col_in, n_col)
    tgt_ref[:, pl.ds(pl.multiple_of(me_r * width, width), width)] = value
    copies += send_row(
        lambda to: piece(tgt_ref, me_r, width), lambda r: piece(tgt_ref, r, width), s3, r3
    )

    number = (iota((n, LANES), 0) * LANES + iota((n, LANES), 1)).astype(F32)
    mine = grid_ref[0] == me.astype(F32)
    before = (iota((LANES, LANES), 0) < iota((LANES, LANES), 1)).astype(BF16)
    rank = jnp.dot(mine.astype(BF16), before, preferred_element_type=F32)
    ids, nexts, id_rows, next_rows = [], [], [], []
    for k in range(2):
        chosen = jnp.logical_and(mine, rank == float(k))
        count = jnp.sum(jnp.where(chosen, 1.0, 0.0), axis=1, keepdims=True)
        one = jnp.sum(jnp.where(chosen, number, 0.0), axis=1, keepdims=True)
        two = jnp.sum(jnp.where(chosen, grid_ref[1], 0.0), axis=1, keepdims=True)
        ids.append(jnp.where(count > 0.5, one, -1.0))
        nexts.append(jnp.where(count > 0.5, two, -2.0))
        id_rows.append(to_row(ids[k], eye))
        next_rows.append(to_row(nexts[k], eye))
    for k in range(2):
        for m in range(2):
            at = (slice(k * n, (k + 1) * n), slice(m * n, (m + 1) * n))
            pair_ref[0, at[0], at[1]] = jnp.where(nexts[k] == id_rows[m], 1.0, 0.0)
            pair_ref[1, at[0], at[1]] = jnp.where(ids[k] == next_rows[m], 1.0, 0.0)

    wait_from(me_r, n_row, lambda r: piece(tgt_ref, r, width), r3)
    for copy in copies:
        copy.wait_send()

    a_ref[...] = jnp.zeros_like(a_ref)
    for h in range(2):
        at = slice(h * half, (h + 1) * half)
        t = [tgt_ref[h * 3 + c : h * 3 + c + 1, :] for c in range(3)]
        rows = []
        for value in t:
            top, middle, low = (part.astype(F32) for part in three_parts(-2.0 * value))
            rows += [top, top, middle, top, low, middle]
        rows += [jnp.ones_like(t[0])] * 3
        square = t[0] * t[0] + t[1] * t[1] + t[2] * t[2] + CORE_SQUARED
        rows += [part.astype(F32) for part in three_parts(square)]
        for k, row in enumerate(rows):
            a_ref[k : k + 1, at] = row

    acc_ref[...] = jnp.zeros_like(acc_ref)
    a = a_ref[...].astype(BF16)

    def add_blocks(first, count):
        b_at = pl.multiple_of(first * 32, 32)
        f_at = pl.multiple_of(first * 16, 16)
        b = jnp.concatenate(
            [b_ref[pl.ds(b_at + 32 * j, 32), :].astype(BF16) for j in range(count)], axis=1
        )
        f = jnp.concatenate(
            [f_ref[pl.ds(f_at + 16 * j, 16), :].astype(BF16) for j in range(count)], axis=1
        )
        q = lax.dot_general(b, a, (((0,), (0,)), ((), ())), preferred_element_type=F32)
        r = lax.rsqrt(q)
        top, low = two_parts(r * r * r)
        acc_ref[...] += jnp.dot(f, top, preferred_element_type=F32) + jnp.dot(
            f, low, preferred_element_type=F32
        )

    def tile(ref, device):
        return ref.at[pl.ds(pl.multiple_of(device * 8, 8), 8), :]

    def start_block(step, carry):
        to = lax.rem(me + step, n)
        pltpu.make_async_remote_copy(
            src_ref=tile(send_ref, to),
            dst_ref=tile(arrived_ref, me),
            send_sem=send_sem,
            recv_sem=recv_sem,
            device_id=(to // n_col, lax.rem(to, n_col)),
            device_id_type=MESH,
        ).start()
        return carry

    turns = slots // CHUNK
    each = n // turns
    own = pl.ds(pl.multiple_of(me * 8, 8), 8)
    arrived_ref[own, :] = send_ref[own, :]
    lax.fori_loop(1, each, start_block, 0)

    def chunk(turn, carry):
        lax.fori_loop((turn + 1) * each, (turn + 2) * each, start_block, 0)
        add_blocks(turn * CHUNK, CHUNK)
        return carry

    lax.fori_loop(0, turns - 1, chunk, 0)
    add_blocks((turns - 1) * CHUNK, CHUNK)

    rest = pl.ds(0, 8 * (n - 1))
    pltpu.make_async_copy(arrived_ref.at[rest], arrived_ref.at[rest], recv_sem).wait()
    pltpu.make_async_copy(send_ref.at[rest], send_ref.at[rest], send_sem).wait()

    y = [
        jnp.concatenate(
            [arrived_ref[pl.ds(2 * c + k, n, stride=8), :] for k in range(2)], axis=0
        )
        for c in range(3)
    ]
    nxt = pick_rows(pair_ref[0].astype(BF16), y)
    prv = pick_rows(pair_ref[1].astype(BF16), y)
    lane = iota((held, LANES), 1)
    arrays = []
    for c in range(3):
        v, nx, pv = y[c], nxt[c], prv[c]
        a1 = jnp.where(lane < LANES - 1, roll(v, -1), roll(nx, -1))
        a2 = jnp.where(lane < LANES - 2, roll(v, -2), roll(nx, -2))
        b1 = jnp.where(lane < 1, roll(pv, 1), roll(v, 1))
        b2 = jnp.where(lane < 2, roll(pv, 2), roll(v, 2))
        sm = (6.0 * v + 4.0 * (a1 + b1) + (a2 + b2)) * 0.0625
        for k in range(2):
            smooth_ref[c, pl.ds(k, n, stride=2), :] = sm[k * n : (k + 1) * n]
        after = (
            6.0 * roll(nx, -1) + 4.0 * (roll(nx, -2) + v) + (roll(nx, -3) + roll(v, 1))
        ) * 0.0625
        ahead = jnp.where(lane < LANES - 1, roll(sm, -1), after)
        arrays += [0.5 * (ahead + sm), ahead - sm]
    pick = jnp.zeros((8, LANES), F32)
    for j, where in enumerate(EDGE_LANES):
        hit = jnp.logical_and(iota((8, LANES), 0) == j, iota((8, LANES), 1) == where)
        pick = pick + jnp.where(hit, 1.0, 0.0)
    stack = jnp.concatenate([part for array in arrays for part in three_parts(array)], axis=0)
    got = lax.dot_general(
        pick.astype(BF16), stack, (((1,), (1,)), ((), ())), preferred_element_type=F32
    )
    got = [
        got[:, 3 * m * held : (3 * m + 1) * held]
        + got[:, (3 * m + 1) * held : (3 * m + 2) * held]
        + got[:, (3 * m + 2) * held : (3 * m + 3) * held]
        for m in range(6)
    ]
    rows, highs, lows = features(got[0::2], got[1::2])
    for k in range(2):
        at = slice(k * n, (k + 1) * n)
        for m, row in enumerate(rows):
            b_ref[pl.ds((slots + k) * 32 + m, 8, stride=64), :] = row[:, at]
        for m in range(6):
            f_ref[pl.ds((slots + k) * 16 + m, 8, stride=32), :] = highs[m][:, at]
            f_ref[pl.ds((slots + k) * 16 + 8 + m, 8, stride=32), :] = lows[m][:, at]
    add_blocks(slots, 2 * len(EDGE_LANES))

    sum_ref[...] = jnp.zeros_like(sum_ref)
    for h in range(2):
        at = slice(h * half, (h + 1) * half)
        t = [tgt_ref[h * 3 + c : h * 3 + c + 1, :] for c in range(3)]
        s = [acc_ref[k : k + 1, at] + acc_ref[8 + k : 9 + k, at] for k in range(6)]
        sum_ref[0:1, at] = scale * (s[1] * t[2] - s[2] * t[1] - s[3])
        sum_ref[1:2, at] = scale * (s[2] * t[0] - s[0] * t[2] - s[4])
        sum_ref[2:3, at] = scale * (s[0] * t[1] - s[1] * t[0] - s[5])
    copies = send_row(lambda to: piece(sum_ref, to, panel), lambda r: row_sum.at[r], s4, r4)
    row_sum[me_r] = sum_ref[:, pl.ds(pl.multiple_of(me_r * panel, panel), panel)]
    wait_from(me_r, n_row, lambda r: row_sum.at[r], r4)
    value = add_up(row_sum, n_row)
    row_total[...] = value
    copies += send_col(row_total, lambda c: col_sum.at[c], s5, r5)
    col_sum[me_c] = value
    wait_from(me_c, n_col, lambda c: col_sum.at[c], r5)
    value = add_up(col_sum, n_col)
    share = vel_ref.shape[1]
    pick = (iota((panel, share), 0) == me_c * share + iota((panel, share), 1)).astype(BF16)
    got = [jnp.dot(part, pick, preferred_element_type=F32) for part in three_parts(value)]
    vel_ref[...] = (got[0] + got[1] + got[2])[:3]
    for copy in copies:
        copy.wait_send()


def shards(n_row, n_col, positions, block_links, panel_points):
    devices = n_row * n_col
    slots, block_len = positions.shape[1:]
    held = 2 * devices
    blocks = block_links.shape[1]
    groups, panel = panel_points.shape
    targets = groups * panel
    width = targets // 2 // n_row
    stored = slots + 2 * 8
    scale = 1.0 / (math.pi * math.sqrt(blocks * block_len))
    whole = pl.BlockSpec(memory_space=pltpu.VMEM)
    dma = pltpu.SemaphoreType.DMA
    smoothed, velocity = pl.pallas_call(
        functools.partial(step_kernel, n_row, n_col, scale),
        out_shape=(
            jax.ShapeDtypeStruct((3, held, block_len), F32),
            jax.ShapeDtypeStruct((3, panel // n_col), F32),
        ),
        in_specs=[whole, whole, whole],
        out_specs=(whole, whole),
        scratch_shapes=[
            pltpu.VMEM((2, devices, slots), F32),
            pltpu.VMEM((8, targets // 2), F32),
            pltpu.VMEM((8, targets // 2), F32),
            pltpu.VMEM((8 * devices, block_len), F32),
            pltpu.VMEM((8 * devices, block_len), F32),
            pltpu.VMEM((stored * 32, LANES), F32),
            pltpu.VMEM((stored * 16, LANES), F32),
            pltpu.VMEM((32, targets), F32),
            pltpu.VMEM((16, targets), F32),
            pltpu.VMEM((2, held, held), F32),
            pltpu.VMEM((8, targets), F32),
            pltpu.VMEM((n_row, 8, width), F32),
            pltpu.VMEM((8, width), F32),
            pltpu.VMEM((n_col, 8, width), F32),
            pltpu.VMEM((n_row, 8, panel), F32),
            pltpu.VMEM((8, panel), F32),
            pltpu.VMEM((n_col, 8, panel), F32),
            dma, dma,
            dma((n_row,)), dma((n_row,)),
            dma((n_col,)), dma((n_col,)),
            dma((n_row,)), dma((n_row,)),
            dma((n_row,)), dma((n_row,)),
            dma((n_col,)), dma((n_col,)),
        ],
        compiler_params=pltpu.CompilerParams(
            vmem_limit_bytes=VMEM_LIMIT, collective_id=0, has_side_effects=True
        ),
        name="step",
    )(positions, block_links, panel_points)
    return smoothed, velocity[None]


def solution(mesh):
    placed = (P(None, ("row", "col"), None), P(), P())
    return jax.shard_map(
        functools.partial(shards, mesh.shape["row"], mesh.shape["col"]),
        mesh=mesh,
        in_specs=placed,
        out_specs=(P(None, ("row", "col"), None), P("row", None, "col")),
        check_vma=False,
    )
```

```python
import functools
import math

import jax
import jax.numpy as jnp
from jax import lax
from jax.experimental import pallas as pl
from jax.experimental.pallas import tpu as pltpu
from jax.sharding import PartitionSpec as P

CORE_SQUARED = 0.01
F32 = jnp.float32
BF16 = jnp.bfloat16
LANES = 128
VMEM_LIMIT = 56 << 20
MESH = pl.DeviceIdType.MESH
CHUNK = 32
TILE = 256
EDGE_LANES = (125, 126, 127, 0, 1)


def iota(shape, axis):
    return lax.broadcasted_iota(jnp.int32, shape, axis)


def three_parts(value):
    high = value.astype(BF16)
    rest = value - high.astype(F32)
    middle = rest.astype(BF16)
    return high, middle, (rest - middle.astype(F32)).astype(BF16)


def two_parts(value):
    high = value.astype(BF16)
    return high, (value - high.astype(F32)).astype(BF16)


def to_column(row, eye):
    return jnp.sum(jnp.where(eye, row, 0.0), axis=1, keepdims=True)


def to_row(column, eye):
    return jnp.sum(jnp.where(eye, column, 0.0), axis=0, keepdims=True)


def pick_rows(chooser, arrays):
    width = arrays[0].shape[1]
    parts = jnp.concatenate([part for array in arrays for part in three_parts(array)], axis=1)
    got = jnp.dot(chooser, parts, preferred_element_type=F32)
    result = []
    for n in range(len(arrays)):
        at = 3 * n * width
        result.append(
            got[:, at : at + width]
            + got[:, at + width : at + 2 * width]
            + got[:, at + 2 * width : at + 3 * width]
        )
    return result


def pick_lanes(lanes, arrays):
    rows = arrays[0].shape[0]
    pick = jnp.zeros((8, LANES), F32)
    for j, where in enumerate(lanes):
        hit = jnp.logical_and(iota((8, LANES), 0) == j, iota((8, LANES), 1) == where)
        pick = pick + jnp.where(hit, 1.0, 0.0)
    stack = jnp.concatenate([part for array in arrays for part in three_parts(array)], axis=0)
    got = lax.dot_general(
        pick.astype(BF16), stack, (((1,), (1,)), ((), ())), preferred_element_type=F32
    )
    return [
        got[:, 3 * m * rows : (3 * m + 1) * rows]
        + got[:, (3 * m + 1) * rows : (3 * m + 2) * rows]
        + got[:, (3 * m + 2) * rows : (3 * m + 3) * rows]
        for m in range(len(arrays))
    ]


def roll(value, shift):
    return pltpu.roll(value, shift % LANES, 1)


def features(centres, segments):
    rows = []
    for c in centres:
        high, middle, low = (part.astype(F32) for part in three_parts(c))
        rows += [high, middle, high, low, high, middle]
    square = centres[0] * centres[0] + centres[1] * centres[1] + centres[2] * centres[2]
    rows += [part.astype(F32) for part in three_parts(square)]
    rows += [jnp.ones_like(square)] * 3
    s, c = segments, centres
    six = [s[0], s[1], s[2]]
    six += [s[1] * c[2] - s[2] * c[1], s[2] * c[0] - s[0] * c[2], s[0] * c[1] - s[1] * c[0]]
    pairs = [two_parts(value) for value in six]
    return rows, [pair[0].astype(F32) for pair in pairs], [pair[1].astype(F32) for pair in pairs]


def step_kernel(
    n_row, n_col, scale, pos_ref, links_ref, panel_ref, smooth_ref, vel_ref,
    grid_ref, part_ref, tgt_ref, send_ref, arrived_ref, b_ref, f_ref, a_ref, acc_ref,
    pair_ref, sum_ref, row_in, total, col_in, row_sum, row_total, col_sum,
    held_ref, out_sem, send_sem, recv_sem, s1, r1, s2, r2, s3, r3, s4, r4, s5, r5,
):
    me_r = lax.axis_index("row")
    me_c = lax.axis_index("col")
    me = me_r * n_col + me_c
    n = n_row * n_col
    slots = pos_ref.shape[1]
    held = 2 * n

    barrier = pltpu.get_barrier_semaphore()
    for step in range(1, n_row):
        to = lax.rem(me_r + step, n_row)
        pl.semaphore_signal(barrier, inc=1, device_id=(to, me_c), device_id_type=MESH)
    for step in range(1, n_col):
        to = lax.rem(me_c + step, n_col)
        pl.semaphore_signal(barrier, inc=1, device_id=(me_r, to), device_id_type=MESH)

    def send_row(source, target, send, recv):
        copies = []
        for step in range(1, n_row):
            to = lax.rem(me_r + step, n_row)
            copy = pltpu.make_async_remote_copy(
                src_ref=source(to),
                dst_ref=target(me_r),
                send_sem=send.at[step],
                recv_sem=recv.at[me_r],
                device_id=(to, me_c),
                device_id_type=MESH,
            )
            copy.start()
            copies.append(copy)
        return copies

    def send_col(source, target, send, recv):
        copies = []
        for step in range(1, n_col):
            to = lax.rem(me_c + step, n_col)
            copy = pltpu.make_async_remote_copy(
                src_ref=source,
                dst_ref=target(me_c),
                send_sem=send.at[step],
                recv_sem=recv.at[me_c],
                device_id=(me_r, to),
                device_id_type=MESH,
            )
            copy.start()
            copies.append(copy)
        return copies

    def wait_from(mine, count, target, recv):
        for step in range(1, count):
            frm = lax.rem(mine + step, count)
            pltpu.make_async_copy(target(frm), target(frm), recv.at[frm]).wait()

    def add_up(ref, count):
        value = ref[0]
        for r in range(1, count):
            value = value + ref[r]
        return value

    eye = iota((slots, LANES), 0) == iota((slots, LANES), 1)
    here = pl.ds(pl.multiple_of(me * slots, LANES), LANES)
    owner_row = links_ref[0:1, here].astype(F32)
    follow_row = links_ref[1:2, here].astype(F32)
    follow_col = to_column(follow_row, eye)
    mine_col = (me * slots + iota((slots, 1), 0)).astype(F32)
    lane_row = iota((1, LANES), 1).astype(F32)

    def look(turn, found):
        at = pl.multiple_of(turn * LANES, LANES)
        row = links_ref[1:2, pl.ds(at, LANES)].astype(F32)
        grid_ref[1, pl.ds(turn, 1), :] = row
        grid_ref[0, pl.ds(turn, 1), :] = links_ref[0:1, pl.ds(at, LANES)].astype(F32)
        number = lane_row + (turn * LANES).astype(F32)
        return found + jnp.where(row == mine_col, number, 0.0)

    precede_col = jnp.sum(
        lax.fori_loop(0, n, look, jnp.zeros((slots, LANES), F32), unroll=8),
        axis=1,
        keepdims=True,
    )
    raw = [pos_ref[c] for c in range(3)]
    lane = iota((slots, LANES), 1)
    inside, wraps = [], []
    for x in raw:
        b1, b2, a1, a2 = roll(x, 1), roll(x, 2), roll(x, -1), roll(x, -2)
        zero = jnp.zeros_like(x)
        wrap = (
            4.0 * (jnp.where(lane < 1, b1, zero) + jnp.where(lane > LANES - 2, a1, zero))
            + (jnp.where(lane < 2, b2, zero) + jnp.where(lane > LANES - 3, a2, zero))
        )
        within = (
            6.0 * x
            + 4.0 * (jnp.where(lane < 1, zero, b1) + jnp.where(lane > LANES - 2, zero, a1))
            + (jnp.where(lane < 2, zero, b2) + jnp.where(lane > LANES - 3, zero, a2))
        )
        inside.append(within * 0.0625)
        wraps.append(wrap * 0.0625)
    parts = jnp.concatenate(three_parts(jnp.concatenate(inside, axis=0)), axis=0)
    high = 3 * slots
    edges = pick_lanes((LANES - 2, LANES - 1, 0, 1), wraps)
    edge_parts = jnp.concatenate([part for edge in edges for part in three_parts(edge)], axis=0)
    panel = panel_ref.shape[1]
    half = tgt_ref.shape[1]
    per_half = half // panel
    part_ref[...] = jnp.zeros_like(part_ref)
    kind = iota((8, panel), 0)
    edge_point = jnp.where(kind < 2, kind + (LANES - 2), jnp.where(kind < 4, kind - 2, -1))
    for r in range(panel_ref.shape[0]):
        flat = panel_ref[r : r + 1, :]
        block = (flat // LANES).astype(F32)
        point = flat % LANES
        one_point = (iota((LANES, panel), 0) == point).astype(BF16)
        got = jnp.dot(parts, one_point, preferred_element_type=F32)
        got = got[:high] + got[high : 2 * high] + got[2 * high :]
        here_mask = block == mine_col
        over = jnp.dot(
            edge_parts, (precede_col == block).astype(BF16), preferred_element_type=F32
        )
        under = jnp.dot(
            edge_parts, (follow_col == block).astype(BF16), preferred_element_type=F32
        )
        beyond = jnp.where(lax.rem(iota(over.shape, 0), 8) < 2, over, under)
        for c in range(3):
            inner = jnp.where(here_mask, got[c * slots : (c + 1) * slots], 0.0)
            outer = beyond[24 * c : 24 * c + 8]
            outer = outer + beyond[24 * c + 8 : 24 * c + 16] + beyond[24 * c + 16 : 24 * c + 24]
            value = jnp.sum(inner, axis=0, keepdims=True) + jnp.sum(
                jnp.where(edge_point == point, outer, 0.0), axis=0, keepdims=True
            )
            row = (r // per_half) * 3 + c
            col = (r % per_half) * panel
            part_ref[row : row + 1, col : col + panel] = value

    width = half // n_row

    def piece(ref, r, size):
        return ref.at[:, pl.ds(pl.multiple_of(r * size, size), size)]

    pl.semaphore_wait(barrier, n_row + n_col - 2)
    copies = send_row(lambda to: piece(part_ref, to, width), lambda r: row_in.at[r], s1, r1)
    row_in[me_r] = part_ref[:, pl.ds(pl.multiple_of(me_r * width, width), width)]

    owner_col = to_column(owner_row, eye)
    earlier = iota((slots, LANES), 0) < iota((slots, LANES), 1)
    same = jnp.logical_and(owner_col == owner_row, earlier)
    rank_row = jnp.sum(jnp.where(same, 1.0, 0.0), axis=0, keepdims=True)
    send_ref[...] = jnp.zeros_like(send_ref)
    to_owner = iota((n, LANES), 0).astype(F32) == owner_row
    for k in range(2):
        chooser = jnp.logical_and(to_owner, rank_row == float(k)).astype(BF16)
        for c, moved in enumerate(pick_rows(chooser, raw)):
            send_ref[pl.ds(2 * c + k, n, stride=8), :] = moved

    wait_from(me_r, n_row, lambda r: row_in.at[r], r1)
    value = add_up(row_in, n_row)
    total[...] = value
    copies += send_col(total, lambda c: col_in.at[c], s2, r2)
    col_in[me_c] = value

    b_ref[...] = jnp.zeros_like(b_ref)
    f_ref[...] = jnp.zeros_like(f_ref)
    inner = jnp.logical_and(lane >= 2, lane < LANES - 3)
    centres, segments = [], []
    for x in raw:
        sm = (6.0 * x + 4.0 * (roll(x, 1) + roll(x, -1)) + (roll(x, 2) + roll(x, -2))) * 0.0625
        ahead = roll(sm, -1)
        segments.append(jnp.where(inner, ahead - sm, 0.0))
        centres.append(0.5 * (ahead + sm))
    rows, highs, lows = features(centres, segments)
    for k, row in enumerate(rows):
        b_ref[pl.ds(k, slots, stride=32), :] = row
    for k in range(6):
        f_ref[pl.ds(k, slots, stride=16), :] = highs[k]
        f_ref[pl.ds(8 + k, slots, stride=16), :] = lows[k]

    wait_from(me_c, n_col, lambda c: col_in.at[c], r2)
    value = add_up(col_in, n_col)
    tgt_ref[:, pl.ds(pl.multiple_of(me_r * width, width), width)] = value
    copies += send_row(
        lambda to: piece(tgt_ref, me_r, width), lambda r: piece(tgt_ref, r, width), s3, r3
    )

    number = (iota((n, LANES), 0) * LANES + iota((n, LANES), 1)).astype(F32)
    mine = grid_ref[0] == me.astype(F32)
    before = (iota((LANES, LANES), 0) < iota((LANES, LANES), 1)).astype(BF16)
    rank = jnp.dot(mine.astype(BF16), before, preferred_element_type=F32)
    ids, nexts, id_rows, next_rows = [], [], [], []
    for k in range(2):
        chosen = jnp.logical_and(mine, rank == float(k))
        count = jnp.sum(jnp.where(chosen, 1.0, 0.0), axis=1, keepdims=True)
        one = jnp.sum(jnp.where(chosen, number, 0.0), axis=1, keepdims=True)
        two = jnp.sum(jnp.where(chosen, grid_ref[1], 0.0), axis=1, keepdims=True)
        ids.append(jnp.where(count > 0.5, one, -1.0))
        nexts.append(jnp.where(count > 0.5, two, -2.0))
        id_rows.append(to_row(ids[k], eye))
        next_rows.append(to_row(nexts[k], eye))
    for k in range(2):
        for m in range(2):
            at = (slice(k * n, (k + 1) * n), slice(m * n, (m + 1) * n))
            pair_ref[0, at[0], at[1]] = jnp.where(nexts[k] == id_rows[m], 1.0, 0.0)
            pair_ref[1, at[0], at[1]] = jnp.where(ids[k] == next_rows[m], 1.0, 0.0)

    wait_from(me_r, n_row, lambda r: piece(tgt_ref, r, width), r3)
    for copy in copies:
        copy.wait_send()

    a_ref[...] = jnp.zeros_like(a_ref)
    for h in range(2):
        at = slice(h * half, (h + 1) * half)
        t = [tgt_ref[h * 3 + c : h * 3 + c + 1, :] for c in range(3)]
        rows = []
        for value in t:
            top, middle, low = (part.astype(F32) for part in three_parts(-2.0 * value))
            rows += [top, top, middle, top, low, middle]
        rows += [jnp.ones_like(t[0])] * 3
        square = t[0] * t[0] + t[1] * t[1] + t[2] * t[2] + CORE_SQUARED
        rows += [part.astype(F32) for part in three_parts(square)]
        for k, row in enumerate(rows):
            a_ref[k : k + 1, at] = row

    acc_ref[...] = jnp.zeros_like(acc_ref)

    def add_blocks(first, count):
        b_at = pl.multiple_of(first * 32, 32)
        f_at = pl.multiple_of(first * 16, 16)
        b = jnp.concatenate(
            [b_ref[pl.ds(b_at + 32 * j, 32), :].astype(BF16) for j in range(count)], axis=1
        )
        f = jnp.concatenate(
            [f_ref[pl.ds(f_at + 16 * j, 16), :].astype(BF16) for j in range(count)], axis=1
        )
        for at in range(0, acc_ref.shape[1], TILE):
            a = a_ref[:, at : at + TILE].astype(BF16)
            q = lax.dot_general(b, a, (((0,), (0,)), ((), ())), preferred_element_type=F32)
            r = lax.rsqrt(q)
            top, low = two_parts(r * r * r)
            acc_ref[:, at : at + TILE] += jnp.dot(f, top, preferred_element_type=F32) + jnp.dot(
                f, low, preferred_element_type=F32
            )

    def tile(ref, device):
        return ref.at[pl.ds(pl.multiple_of(device * 8, 8), 8), :]

    def start_block(step):
        to = lax.rem(me + step, n)
        pltpu.make_async_remote_copy(
            src_ref=tile(send_ref, to),
            dst_ref=tile(arrived_ref, me),
            send_sem=send_sem,
            recv_sem=recv_sem,
            device_id=(to // n_col, lax.rem(to, n_col)),
            device_id_type=MESH,
        ).start()

    turns = slots // CHUNK
    each = (n - 1) // (turns - 1)
    own = pl.ds(pl.multiple_of(me * 8, 8), 8)
    arrived_ref[own, :] = send_ref[own, :]
    for step in range(each * (turns - 1) + 1, n):
        start_block(step)

    def chunk(turn, carry):
        for j in range(each):
            start_block(turn * each + (j + 1))
        add_blocks(turn * CHUNK, CHUNK)
        return carry

    lax.fori_loop(0, turns - 1, chunk, 0)
    add_blocks((turns - 1) * CHUNK, CHUNK)

    rest = pl.ds(0, 8 * (n - 1))
    pltpu.make_async_copy(arrived_ref.at[rest], arrived_ref.at[rest], recv_sem).wait()
    pltpu.make_async_copy(send_ref.at[rest], send_ref.at[rest], send_sem).wait()

    y = [
        jnp.concatenate(
            [arrived_ref[pl.ds(2 * c + k, n, stride=8), :] for k in range(2)], axis=0
        )
        for c in range(3)
    ]
    nxt = pick_rows(pair_ref[0].astype(BF16), y)
    prv = pick_rows(pair_ref[1].astype(BF16), y)
    lane = iota((held, LANES), 1)
    arrays = []
    for c in range(3):
        v, nx, pv = y[c], nxt[c], prv[c]
        a1 = jnp.where(lane < LANES - 1, roll(v, -1), roll(nx, -1))
        a2 = jnp.where(lane < LANES - 2, roll(v, -2), roll(nx, -2))
        b1 = jnp.where(lane < 1, roll(pv, 1), roll(v, 1))
        b2 = jnp.where(lane < 2, roll(pv, 2), roll(v, 2))
        sm = (6.0 * v + 4.0 * (a1 + b1) + (a2 + b2)) * 0.0625
        for k in range(2):
            held_ref[c, pl.ds(k, n, stride=2), :] = sm[k * n : (k + 1) * n]
        after = (
            6.0 * roll(nx, -1) + 4.0 * (roll(nx, -2) + v) + (roll(nx, -3) + roll(v, 1))
        ) * 0.0625
        ahead = jnp.where(lane < LANES - 1, roll(sm, -1), after)
        arrays += [0.5 * (ahead + sm), ahead - sm]
    got = pick_lanes(EDGE_LANES, arrays)
    written = pltpu.make_async_copy(held_ref, smooth_ref, out_sem)
    written.start()
    rows, highs, lows = features(got[0::2], got[1::2])
    for k in range(2):
        at = slice(k * n, (k + 1) * n)
        for m, row in enumerate(rows):
            b_ref[pl.ds((slots + k) * 32 + m, 8, stride=64), :] = row[:, at]
        for m in range(6):
            f_ref[pl.ds((slots + k) * 16 + m, 8, stride=32), :] = highs[m][:, at]
            f_ref[pl.ds((slots + k) * 16 + 8 + m, 8, stride=32), :] = lows[m][:, at]
    add_blocks(slots, 2 * len(EDGE_LANES))

    sum_ref[...] = jnp.zeros_like(sum_ref)
    for h in range(2):
        at = slice(h * half, (h + 1) * half)
        t = [tgt_ref[h * 3 + c : h * 3 + c + 1, :] for c in range(3)]
        s = [acc_ref[k : k + 1, at] + acc_ref[8 + k : 9 + k, at] for k in range(6)]
        v = [
            scale * (s[1] * t[2] - s[2] * t[1] - s[3]),
            scale * (s[2] * t[0] - s[0] * t[2] - s[4]),
            scale * (s[0] * t[1] - s[1] * t[0] - s[5]),
        ]
        for m in range(half // LANES):
            group = (h * half + m * LANES) // panel
            for c in range(3):
                row = 2 * c + m % 2
                sum_ref[row : row + 1, group * LANES : (group + 1) * LANES] = v[c][
                    :, m * LANES : (m + 1) * LANES
                ]
    copies = send_row(lambda to: piece(sum_ref, to, LANES), lambda r: row_sum.at[r], s4, r4)
    row_sum[me_r] = sum_ref[:, pl.ds(pl.multiple_of(me_r * LANES, LANES), LANES)]
    wait_from(me_r, n_row, lambda r: row_sum.at[r], r4)
    value = add_up(row_sum, n_row)
    row_total[...] = value
    copies += send_col(row_total, lambda c: col_sum.at[c], s5, r5)
    col_sum[me_c] = value
    wait_from(me_c, n_col, lambda c: col_sum.at[c], r5)
    value = add_up(col_sum, n_col)
    share = vel_ref.shape[2]
    per_row = LANES // share
    first = lax.rem(me_c, per_row) * share
    pick = (iota((LANES, share), 0) == first + iota((LANES, share), 1)).astype(BF16)
    got = [jnp.dot(part, pick, preferred_element_type=F32) for part in three_parts(value)]
    got = got[0] + got[1] + got[2]
    lower = (iota((1, share), 1) + me_c) < iota((1, share), 1) + per_row
    for c in range(3):
        vel_ref[c] = jnp.where(lower, got[2 * c : 2 * c + 1], got[2 * c + 1 : 2 * c + 2])
    for copy in copies:
        copy.wait_send()
    written.wait()


def shards(n_row, n_col, positions, block_links, panel_points):
    devices = n_row * n_col
    slots, block_len = positions.shape[1:]
    held = 2 * devices
    blocks = block_links.shape[1]
    groups, panel = panel_points.shape
    targets = groups * panel
    width = targets // 2 // n_row
    stored = slots + 2 * 8
    scale = 1.0 / (math.pi * math.sqrt(blocks * block_len))
    whole = pl.BlockSpec(memory_space=pltpu.VMEM)
    dma = pltpu.SemaphoreType.DMA
    smoothed, velocity = pl.pallas_call(
        functools.partial(step_kernel, n_row, n_col, scale),
        out_shape=(
            jax.ShapeDtypeStruct((3, held, block_len), F32),
            jax.ShapeDtypeStruct((3, 1, panel // n_col), F32),
        ),
        in_specs=[whole, whole, whole],
        out_specs=(pl.BlockSpec(memory_space=pl.ANY), whole),
        scratch_shapes=[
            pltpu.VMEM((2, devices, slots), F32),
            pltpu.VMEM((8, targets // 2), F32),
            pltpu.VMEM((8, targets // 2), F32),
            pltpu.VMEM((8 * devices, block_len), F32),
            pltpu.VMEM((8 * devices, block_len), F32),
            pltpu.VMEM((stored * 32, LANES), F32),
            pltpu.VMEM((stored * 16, LANES), F32),
            pltpu.VMEM((32, targets), F32),
            pltpu.VMEM((16, targets), F32),
            pltpu.VMEM((2, held, held), F32),
            pltpu.VMEM((8, groups * LANES), F32),
            pltpu.VMEM((n_row, 8, width), F32),
            pltpu.VMEM((8, width), F32),
            pltpu.VMEM((n_col, 8, width), F32),
            pltpu.VMEM((n_row, 8, LANES), F32),
            pltpu.VMEM((8, LANES), F32),
            pltpu.VMEM((n_col, 8, LANES), F32),
            pltpu.VMEM((3, held, block_len), F32),
            dma, dma, dma,
            dma((n_row,)), dma((n_row,)),
            dma((n_col,)), dma((n_col,)),
            dma((n_row,)), dma((n_row,)),
            dma((n_row,)), dma((n_row,)),
            dma((n_col,)), dma((n_col,)),
        ],
        compiler_params=pltpu.CompilerParams(
            vmem_limit_bytes=VMEM_LIMIT, collective_id=0, has_side_effects=True
        ),
        name="step",
    )(positions, block_links, panel_points)
    return smoothed, jnp.transpose(velocity, (1, 0, 2))


def solution(mesh):
    placed = (P(None, ("row", "col"), None), P(), P())
    return jax.shard_map(
        functools.partial(shards, mesh.shape["row"], mesh.shape["col"]),
        mesh=mesh,
        in_specs=placed,
        out_specs=(P(None, ("row", "col"), None), P("row", None, "col")),
        check_vma=False,
    )
```

```python
import functools
import math

import jax
import jax.numpy as jnp
from jax import lax
from jax.experimental import pallas as pl
from jax.experimental.pallas import tpu as pltpu
from jax.sharding import PartitionSpec as P

CORE_SQUARED = 0.01
F32 = jnp.float32
BF16 = jnp.bfloat16
LANES = 128
VMEM_LIMIT = 56 << 20
MESH = pl.DeviceIdType.MESH
CHUNK = 32
EDGE_LANES = (125, 126, 127, 0, 1)


def iota(shape, axis):
    return lax.broadcasted_iota(jnp.int32, shape, axis)


def three_parts(value):
    high = value.astype(BF16)
    rest = value - high.astype(F32)
    middle = rest.astype(BF16)
    return high, middle, (rest - middle.astype(F32)).astype(BF16)


def two_parts(value):
    high = value.astype(BF16)
    return high, (value - high.astype(F32)).astype(BF16)


def to_column(row, eye):
    return jnp.sum(jnp.where(eye, row, 0.0), axis=1, keepdims=True)


def to_row(column, eye):
    return jnp.sum(jnp.where(eye, column, 0.0), axis=0, keepdims=True)


def pick_rows(chooser, arrays):
    width = arrays[0].shape[1]
    parts = jnp.concatenate([part for array in arrays for part in three_parts(array)], axis=1)
    got = jnp.dot(chooser, parts, preferred_element_type=F32)
    result = []
    for n in range(len(arrays)):
        at = 3 * n * width
        result.append(
            got[:, at : at + width]
            + got[:, at + width : at + 2 * width]
            + got[:, at + 2 * width : at + 3 * width]
        )
    return result


def pick_lanes(lanes, arrays):
    rows = arrays[0].shape[0]
    pick = jnp.zeros((8, LANES), F32)
    for j, where in enumerate(lanes):
        hit = jnp.logical_and(iota((8, LANES), 0) == j, iota((8, LANES), 1) == where)
        pick = pick + jnp.where(hit, 1.0, 0.0)
    stack = jnp.concatenate([part for array in arrays for part in three_parts(array)], axis=0)
    got = lax.dot_general(
        pick.astype(BF16), stack, (((1,), (1,)), ((), ())), preferred_element_type=F32
    )
    return [
        got[:, 3 * m * rows : (3 * m + 1) * rows]
        + got[:, (3 * m + 1) * rows : (3 * m + 2) * rows]
        + got[:, (3 * m + 2) * rows : (3 * m + 3) * rows]
        for m in range(len(arrays))
    ]


def roll(value, shift):
    return pltpu.roll(value, shift % LANES, 1)


def features(centres, segments):
    rows = []
    for c in centres:
        high, middle, low = (part.astype(F32) for part in three_parts(c))
        rows += [high, middle, high, low, high, middle]
    square = centres[0] * centres[0] + centres[1] * centres[1] + centres[2] * centres[2]
    rows += [part.astype(F32) for part in three_parts(square)]
    rows += [jnp.ones_like(square)] * 3
    s, c = segments, centres
    six = [s[0], s[1], s[2]]
    six += [s[1] * c[2] - s[2] * c[1], s[2] * c[0] - s[0] * c[2], s[0] * c[1] - s[1] * c[0]]
    pairs = [two_parts(value) for value in six]
    return rows, [pair[0].astype(F32) for pair in pairs], [pair[1].astype(F32) for pair in pairs]


def step_kernel(
    n_row, n_col, scale, pos_ref, links_ref, panel_ref, smooth_ref, vel_ref,
    grid_ref, part_ref, tgt_ref, send_ref, arrived_ref, b_ref, f_ref, a_ref, acc_ref,
    pair_ref, sum_ref, row_in, total, col_in, row_sum, row_total, col_sum,
    held_ref, out_sem, send_sem, recv_sem, s1, r1, s2, r2, s3, r3, s4, r4, s5, r5,
):
    me_r = lax.axis_index("row")
    me_c = lax.axis_index("col")
    me = me_r * n_col + me_c
    n = n_row * n_col
    slots = pos_ref.shape[1]
    held = 2 * n

    barrier = pltpu.get_barrier_semaphore()
    for step in range(1, n_row):
        to = lax.rem(me_r + step, n_row)
        pl.semaphore_signal(barrier, inc=1, device_id=(to, me_c), device_id_type=MESH)
    for step in range(1, n_col):
        to = lax.rem(me_c + step, n_col)
        pl.semaphore_signal(barrier, inc=1, device_id=(me_r, to), device_id_type=MESH)

    def send_row(source, target, send, recv):
        copies = []
        for step in range(1, n_row):
            to = lax.rem(me_r + step, n_row)
            copy = pltpu.make_async_remote_copy(
                src_ref=source(to),
                dst_ref=target(me_r),
                send_sem=send.at[step],
                recv_sem=recv.at[me_r],
                device_id=(to, me_c),
                device_id_type=MESH,
            )
            copy.start()
            copies.append(copy)
        return copies

    def send_col(source, target, send, recv):
        copies = []
        for step in range(1, n_col):
            to = lax.rem(me_c + step, n_col)
            copy = pltpu.make_async_remote_copy(
                src_ref=source,
                dst_ref=target(me_c),
                send_sem=send.at[step],
                recv_sem=recv.at[me_c],
                device_id=(me_r, to),
                device_id_type=MESH,
            )
            copy.start()
            copies.append(copy)
        return copies

    def wait_from(mine, count, target, recv):
        for step in range(1, count):
            frm = lax.rem(mine + step, count)
            pltpu.make_async_copy(target(frm), target(frm), recv.at[frm]).wait()

    def add_up(ref, count):
        value = ref[0]
        for r in range(1, count):
            value = value + ref[r]
        return value

    eye = iota((slots, LANES), 0) == iota((slots, LANES), 1)
    here = pl.ds(pl.multiple_of(me * slots, LANES), LANES)
    owner_row = links_ref[0:1, here].astype(F32)
    follow_row = links_ref[1:2, here].astype(F32)
    follow_col = to_column(follow_row, eye)
    mine_col = (me * slots + iota((slots, 1), 0)).astype(F32)
    lane_row = iota((1, LANES), 1).astype(F32)

    def look(turn, found):
        at = pl.multiple_of(turn * LANES, LANES)
        row = links_ref[1:2, pl.ds(at, LANES)].astype(F32)
        grid_ref[1, pl.ds(turn, 1), :] = row
        grid_ref[0, pl.ds(turn, 1), :] = links_ref[0:1, pl.ds(at, LANES)].astype(F32)
        number = lane_row + (turn * LANES).astype(F32)
        return found + jnp.where(row == mine_col, number, 0.0)

    precede_col = jnp.sum(
        lax.fori_loop(0, n, look, jnp.zeros((slots, LANES), F32), unroll=8),
        axis=1,
        keepdims=True,
    )
    raw = [pos_ref[c] for c in range(3)]
    lane = iota((slots, LANES), 1)
    inside, wraps = [], []
    for x in raw:
        b1, b2, a1, a2 = roll(x, 1), roll(x, 2), roll(x, -1), roll(x, -2)
        zero = jnp.zeros_like(x)
        wrap = (
            4.0 * (jnp.where(lane < 1, b1, zero) + jnp.where(lane > LANES - 2, a1, zero))
            + (jnp.where(lane < 2, b2, zero) + jnp.where(lane > LANES - 3, a2, zero))
        )
        within = (
            6.0 * x
            + 4.0 * (jnp.where(lane < 1, zero, b1) + jnp.where(lane > LANES - 2, zero, a1))
            + (jnp.where(lane < 2, zero, b2) + jnp.where(lane > LANES - 3, zero, a2))
        )
        inside.append(within * 0.0625)
        wraps.append(wrap * 0.0625)
    parts = jnp.concatenate(three_parts(jnp.concatenate(inside, axis=0)), axis=0)
    high = 3 * slots
    edges = pick_lanes((LANES - 2, LANES - 1, 0, 1), wraps)
    edge_parts = jnp.concatenate([part for edge in edges for part in three_parts(edge)], axis=0)
    panel = panel_ref.shape[1]
    part_ref[...] = jnp.zeros_like(part_ref)
    kind = iota((8, panel), 0)
    edge_point = jnp.where(kind < 2, kind + (LANES - 2), jnp.where(kind < 4, kind - 2, -1))
    for r in range(panel_ref.shape[0]):
        flat = panel_ref[r : r + 1, :]
        block = (flat // LANES).astype(F32)
        point = flat % LANES
        one_point = (iota((LANES, panel), 0) == point).astype(BF16)
        got = jnp.dot(parts, one_point, preferred_element_type=F32)
        got = got[:high] + got[high : 2 * high] + got[2 * high :]
        here_mask = block == mine_col
        over = jnp.dot(
            edge_parts, (precede_col == block).astype(BF16), preferred_element_type=F32
        )
        under = jnp.dot(
            edge_parts, (follow_col == block).astype(BF16), preferred_element_type=F32
        )
        beyond = jnp.where(lax.rem(iota(over.shape, 0), 8) < 2, over, under)
        for c in range(3):
            inner = jnp.where(here_mask, got[c * slots : (c + 1) * slots], 0.0)
            outer = beyond[24 * c : 24 * c + 8]
            outer = outer + beyond[24 * c + 8 : 24 * c + 16] + beyond[24 * c + 16 : 24 * c + 24]
            value = jnp.sum(inner, axis=0, keepdims=True) + jnp.sum(
                jnp.where(edge_point == point, outer, 0.0), axis=0, keepdims=True
            )
            for h in range(2):
                part_ref[2 * c + h : 2 * c + h + 1, r * LANES : (r + 1) * LANES] = value[
                    :, h * LANES : (h + 1) * LANES
                ]

    width = LANES

    def lanes(r, size):
        return pl.ds(pl.multiple_of(r * size, size), size)

    def piece(ref, r, size):
        return ref.at[:, lanes(r, size)]

    pl.semaphore_wait(barrier, n_row + n_col - 2)
    copies = send_row(lambda to: piece(part_ref, to, width), lambda r: row_in.at[r], s1, r1)
    row_in[me_r] = part_ref[:, pl.ds(pl.multiple_of(me_r * width, width), width)]

    owner_col = to_column(owner_row, eye)
    earlier = iota((slots, LANES), 0) < iota((slots, LANES), 1)
    same = jnp.logical_and(owner_col == owner_row, earlier)
    rank_row = jnp.sum(jnp.where(same, 1.0, 0.0), axis=0, keepdims=True)
    send_ref[...] = jnp.zeros_like(send_ref)
    to_owner = iota((n, LANES), 0).astype(F32) == owner_row
    for k in range(2):
        chooser = jnp.logical_and(to_owner, rank_row == float(k)).astype(BF16)
        for c, moved in enumerate(pick_rows(chooser, raw)):
            send_ref[pl.ds(2 * c + k, n, stride=8), :] = moved

    wait_from(me_r, n_row, lambda r: row_in.at[r], r1)
    value = add_up(row_in, n_row)
    total[...] = value
    copies += send_col(total, lambda c: col_in.at[c], s2, r2)
    col_in[me_c] = value

    b_ref[...] = jnp.zeros_like(b_ref)
    f_ref[...] = jnp.zeros_like(f_ref)
    inner = jnp.logical_and(lane >= 2, lane < LANES - 3)
    centres, segments = [], []
    for x in raw:
        sm = (6.0 * x + 4.0 * (roll(x, 1) + roll(x, -1)) + (roll(x, 2) + roll(x, -2))) * 0.0625
        ahead = roll(sm, -1)
        segments.append(jnp.where(inner, ahead - sm, 0.0))
        centres.append(0.5 * (ahead + sm))
    rows, highs, lows = features(centres, segments)
    for k, row in enumerate(rows):
        b_ref[pl.ds(k, slots, stride=32), :] = row
    for k in range(6):
        f_ref[pl.ds(k, slots, stride=16), :] = highs[k]
        f_ref[pl.ds(8 + k, slots, stride=16), :] = lows[k]

    wait_from(me_c, n_col, lambda c: col_in.at[c], r2)
    value = add_up(col_in, n_col)
    tgt_ref[:, pl.ds(pl.multiple_of(me_r * width, width), width)] = value
    copies += send_row(
        lambda to: piece(tgt_ref, me_r, width), lambda r: piece(tgt_ref, r, width), s3, r3
    )

    number = (iota((n, LANES), 0) * LANES + iota((n, LANES), 1)).astype(F32)
    mine = grid_ref[0] == me.astype(F32)
    before = (iota((LANES, LANES), 0) < iota((LANES, LANES), 1)).astype(BF16)
    rank = jnp.dot(mine.astype(BF16), before, preferred_element_type=F32)
    ids, nexts, id_rows, next_rows = [], [], [], []
    for k in range(2):
        chosen = jnp.logical_and(mine, rank == float(k))
        count = jnp.sum(jnp.where(chosen, 1.0, 0.0), axis=1, keepdims=True)
        one = jnp.sum(jnp.where(chosen, number, 0.0), axis=1, keepdims=True)
        two = jnp.sum(jnp.where(chosen, grid_ref[1], 0.0), axis=1, keepdims=True)
        ids.append(jnp.where(count > 0.5, one, -1.0))
        nexts.append(jnp.where(count > 0.5, two, -2.0))
        id_rows.append(to_row(ids[k], eye))
        next_rows.append(to_row(nexts[k], eye))
    for k in range(2):
        for m in range(2):
            at = (slice(k * n, (k + 1) * n), slice(m * n, (m + 1) * n))
            pair_ref[0, at[0], at[1]] = jnp.where(nexts[k] == id_rows[m], 1.0, 0.0)
            pair_ref[1, at[0], at[1]] = jnp.where(ids[k] == next_rows[m], 1.0, 0.0)

    def aim(r):
        value = tgt_ref[:, lanes(r, LANES)]
        top, middle, low = (part.astype(F32) for part in three_parts(-2.0 * value))
        square = value * value
        for h in range(2):
            at = pl.ds(pl.multiple_of(r * panel + h * LANES, LANES), LANES)
            k = 0
            for c in range(3):
                for part in (top, top, middle, top, low, middle):
                    a_ref[k : k + 1, at] = part[2 * c + h : 2 * c + h + 1]
                    k += 1
            a_ref[k : k + 3, at] = jnp.ones((3, LANES), F32)
            total_square = square[h : h + 1] + square[2 + h : 3 + h] + square[4 + h : 5 + h]
            for m, part in enumerate(three_parts(total_square + CORE_SQUARED)):
                a_ref[k + 3 + m : k + 4 + m, at] = part.astype(F32)

    def add_blocks(first, count, panels):
        b_at = pl.multiple_of(first * 32, 32)
        f_at = pl.multiple_of(first * 16, 16)
        b = jnp.concatenate(
            [b_ref[pl.ds(b_at + 32 * j, 32), :].astype(BF16) for j in range(count)], axis=1
        )
        f = jnp.concatenate(
            [f_ref[pl.ds(f_at + 16 * j, 16), :].astype(BF16) for j in range(count)], axis=1
        )
        for r in panels:
            at = lanes(r, panel)
            a = a_ref[:, at].astype(BF16)
            q = lax.dot_general(b, a, (((0,), (0,)), ((), ())), preferred_element_type=F32)
            root = lax.rsqrt(q)
            top, low = two_parts(root * root * root)
            acc_ref[:, at] += jnp.dot(f, top, preferred_element_type=F32) + jnp.dot(
                f, low, preferred_element_type=F32
            )

    def velocity_of(r):
        value = tgt_ref[:, lanes(r, LANES)]
        for h in range(2):
            at = pl.ds(pl.multiple_of(r * panel + h * LANES, LANES), LANES)
            t = [value[2 * c + h : 2 * c + h + 1] for c in range(3)]
            s = [acc_ref[k : k + 1, at] + acc_ref[8 + k : 9 + k, at] for k in range(6)]
            v = [
                scale * (s[1] * t[2] - s[2] * t[1] - s[3]),
                scale * (s[2] * t[0] - s[0] * t[2] - s[4]),
                scale * (s[0] * t[1] - s[1] * t[0] - s[5]),
            ]
            for c in range(3):
                sum_ref[2 * c + h : 2 * c + h + 1, lanes(r, LANES)] = v[c]

    others = [lax.rem(me_r + k, n_row) for k in range(1, n_row)]
    acc_ref[...] = jnp.zeros_like(acc_ref)
    sum_ref[...] = jnp.zeros_like(sum_ref)
    a_ref[...] = jnp.zeros_like(a_ref)
    aim(me_r)
    for first in range(0, slots // 2, CHUNK // 2):
        add_blocks(first, CHUNK // 2, [me_r])
    wait_from(me_r, n_row, lambda r: piece(tgt_ref, r, width), r3)
    for copy in copies:
        copy.wait_send()
    for r in others:
        aim(r)

    def tile(ref, device):
        return ref.at[pl.ds(pl.multiple_of(device * 8, 8), 8), :]

    def start_block(step):
        to = lax.rem(me + step, n)
        pltpu.make_async_remote_copy(
            src_ref=tile(send_ref, to),
            dst_ref=tile(arrived_ref, me),
            send_sem=send_sem,
            recv_sem=recv_sem,
            device_id=(to // n_col, lax.rem(to, n_col)),
            device_id_type=MESH,
        ).start()

    turns = slots // CHUNK
    each = (n - 1) // turns
    own = pl.ds(pl.multiple_of(me * 8, 8), 8)
    arrived_ref[own, :] = send_ref[own, :]
    for step in range(each * turns + 1, n):
        start_block(step)

    def chunk(turn, carry):
        for j in range(each):
            start_block(turn * each + (j + 1))
        add_blocks(turn * CHUNK, CHUNK, others)
        return carry

    lax.fori_loop(0, turns, chunk, 0)

    rest = pl.ds(0, 8 * (n - 1))
    pltpu.make_async_copy(arrived_ref.at[rest], arrived_ref.at[rest], recv_sem).wait()
    pltpu.make_async_copy(send_ref.at[rest], send_ref.at[rest], send_sem).wait()

    y = [
        jnp.concatenate(
            [arrived_ref[pl.ds(2 * c + k, n, stride=8), :] for k in range(2)], axis=0
        )
        for c in range(3)
    ]
    nxt = pick_rows(pair_ref[0].astype(BF16), y)
    prv = pick_rows(pair_ref[1].astype(BF16), y)
    lane = iota((held, LANES), 1)
    arrays = []
    for c in range(3):
        v, nx, pv = y[c], nxt[c], prv[c]
        a1 = jnp.where(lane < LANES - 1, roll(v, -1), roll(nx, -1))
        a2 = jnp.where(lane < LANES - 2, roll(v, -2), roll(nx, -2))
        b1 = jnp.where(lane < 1, roll(pv, 1), roll(v, 1))
        b2 = jnp.where(lane < 2, roll(pv, 2), roll(v, 2))
        sm = (6.0 * v + 4.0 * (a1 + b1) + (a2 + b2)) * 0.0625
        for k in range(2):
            held_ref[c, pl.ds(k, n, stride=2), :] = sm[k * n : (k + 1) * n]
        after = (
            6.0 * roll(nx, -1) + 4.0 * (roll(nx, -2) + v) + (roll(nx, -3) + roll(v, 1))
        ) * 0.0625
        ahead = jnp.where(lane < LANES - 1, roll(sm, -1), after)
        arrays += [0.5 * (ahead + sm), ahead - sm]
    got = pick_lanes(EDGE_LANES, arrays)
    written = pltpu.make_async_copy(held_ref, smooth_ref, out_sem)
    written.start()
    rows, highs, lows = features(got[0::2], got[1::2])
    for k in range(2):
        at = slice(k * n, (k + 1) * n)
        for m, row in enumerate(rows):
            b_ref[pl.ds((slots + k) * 32 + m, 8, stride=64), :] = row[:, at]
        for m in range(6):
            f_ref[pl.ds((slots + k) * 16 + m, 8, stride=32), :] = highs[m][:, at]
            f_ref[pl.ds((slots + k) * 16 + 8 + m, 8, stride=32), :] = lows[m][:, at]
    add_blocks(slots, 2 * len(EDGE_LANES), others)

    for r in others:
        velocity_of(r)
    copies = send_row(lambda to: piece(sum_ref, to, LANES), lambda r: row_sum.at[r], s4, r4)
    for first in range(slots // 2, slots, CHUNK // 2):
        add_blocks(first, CHUNK // 2, [me_r])
    add_blocks(slots, 2 * len(EDGE_LANES), [me_r])
    velocity_of(me_r)
    row_sum[me_r] = sum_ref[:, pl.ds(pl.multiple_of(me_r * LANES, LANES), LANES)]
    wait_from(me_r, n_row, lambda r: row_sum.at[r], r4)
    value = add_up(row_sum, n_row)
    row_total[...] = value
    copies += send_col(row_total, lambda c: col_sum.at[c], s5, r5)
    col_sum[me_c] = value
    wait_from(me_c, n_col, lambda c: col_sum.at[c], r5)
    value = add_up(col_sum, n_col)
    share = vel_ref.shape[2]
    per_row = LANES // share
    first = lax.rem(me_c, per_row) * share
    pick = (iota((LANES, share), 0) == first + iota((LANES, share), 1)).astype(BF16)
    got = [jnp.dot(part, pick, preferred_element_type=F32) for part in three_parts(value)]
    got = got[0] + got[1] + got[2]
    lower = (iota((1, share), 1) + me_c) < iota((1, share), 1) + per_row
    for c in range(3):
        vel_ref[c] = jnp.where(lower, got[2 * c : 2 * c + 1], got[2 * c + 1 : 2 * c + 2])
    for copy in copies:
        copy.wait_send()
    written.wait()


def shards(n_row, n_col, positions, block_links, panel_points):
    devices = n_row * n_col
    slots, block_len = positions.shape[1:]
    held = 2 * devices
    blocks = block_links.shape[1]
    groups, panel = panel_points.shape
    targets = groups * panel
    width = LANES
    stored = slots + 2 * 8
    scale = 1.0 / (math.pi * math.sqrt(blocks * block_len))
    whole = pl.BlockSpec(memory_space=pltpu.VMEM)
    dma = pltpu.SemaphoreType.DMA
    smoothed, velocity = pl.pallas_call(
        functools.partial(step_kernel, n_row, n_col, scale),
        out_shape=(
            jax.ShapeDtypeStruct((3, held, block_len), F32),
            jax.ShapeDtypeStruct((3, 1, panel // n_col), F32),
        ),
        in_specs=[whole, whole, whole],
        out_specs=(pl.BlockSpec(memory_space=pl.ANY), whole),
        scratch_shapes=[
            pltpu.VMEM((2, devices, slots), F32),
            pltpu.VMEM((8, groups * LANES), F32),
            pltpu.VMEM((8, groups * LANES), F32),
            pltpu.VMEM((8 * devices, block_len), F32),
            pltpu.VMEM((8 * devices, block_len), F32),
            pltpu.VMEM((stored * 32, LANES), F32),
            pltpu.VMEM((stored * 16, LANES), F32),
            pltpu.VMEM((32, targets), F32),
            pltpu.VMEM((16, targets), F32),
            pltpu.VMEM((2, held, held), F32),
            pltpu.VMEM((8, groups * LANES), F32),
            pltpu.VMEM((n_row, 8, width), F32),
            pltpu.VMEM((8, width), F32),
            pltpu.VMEM((n_col, 8, width), F32),
            pltpu.VMEM((n_row, 8, LANES), F32),
            pltpu.VMEM((8, LANES), F32),
            pltpu.VMEM((n_col, 8, LANES), F32),
            pltpu.VMEM((3, held, block_len), F32),
            dma, dma, dma,
            dma((n_row,)), dma((n_row,)),
            dma((n_col,)), dma((n_col,)),
            dma((n_row,)), dma((n_row,)),
            dma((n_row,)), dma((n_row,)),
            dma((n_col,)), dma((n_col,)),
        ],
        compiler_params=pltpu.CompilerParams(
            vmem_limit_bytes=VMEM_LIMIT, collective_id=0, has_side_effects=True
        ),
        name="step",
    )(positions, block_links, panel_points)
    return smoothed, jnp.transpose(velocity, (1, 0, 2))


def solution(mesh):
    placed = (P(None, ("row", "col"), None), P(), P())
    return jax.shard_map(
        functools.partial(shards, mesh.shape["row"], mesh.shape["col"]),
        mesh=mesh,
        in_specs=placed,
        out_specs=(P(None, ("row", "col"), None), P("row", None, "col")),
        check_vma=False,
    )
```

```python
import functools
import math

import jax
import jax.numpy as jnp
from jax import lax
from jax.experimental import pallas as pl
from jax.experimental.pallas import tpu as pltpu
from jax.sharding import PartitionSpec as P

CORE_SQUARED = 0.01
F32 = jnp.float32
BF16 = jnp.bfloat16
LANES = 128
VMEM_LIMIT = 56 << 20
MESH = pl.DeviceIdType.MESH
CHUNK = 32
EDGE_LANES = (125, 126, 127, 0, 1)


def iota(shape, axis):
    return lax.broadcasted_iota(jnp.int32, shape, axis)


def three_parts(value):
    high = value.astype(BF16)
    rest = value - high.astype(F32)
    middle = rest.astype(BF16)
    return high, middle, (rest - middle.astype(F32)).astype(BF16)


def two_parts(value):
    high = value.astype(BF16)
    return high, (value - high.astype(F32)).astype(BF16)


def to_column(row, eye):
    return jnp.sum(jnp.where(eye, row, 0.0), axis=1, keepdims=True)


def to_row(column, eye):
    return jnp.sum(jnp.where(eye, column, 0.0), axis=0, keepdims=True)


def pick_rows(chooser, arrays):
    width = arrays[0].shape[1]
    parts = jnp.concatenate([part for array in arrays for part in three_parts(array)], axis=1)
    got = jnp.dot(chooser, parts, preferred_element_type=F32)
    result = []
    for n in range(len(arrays)):
        at = 3 * n * width
        result.append(
            got[:, at : at + width]
            + got[:, at + width : at + 2 * width]
            + got[:, at + 2 * width : at + 3 * width]
        )
    return result


def pick_lanes(lanes, arrays):
    rows = arrays[0].shape[0]
    pick = jnp.zeros((8, LANES), F32)
    for j, where in enumerate(lanes):
        hit = jnp.logical_and(iota((8, LANES), 0) == j, iota((8, LANES), 1) == where)
        pick = pick + jnp.where(hit, 1.0, 0.0)
    stack = jnp.concatenate([part for array in arrays for part in three_parts(array)], axis=0)
    got = lax.dot_general(
        pick.astype(BF16), stack, (((1,), (1,)), ((), ())), preferred_element_type=F32
    )
    return [
        got[:, 3 * m * rows : (3 * m + 1) * rows]
        + got[:, (3 * m + 1) * rows : (3 * m + 2) * rows]
        + got[:, (3 * m + 2) * rows : (3 * m + 3) * rows]
        for m in range(len(arrays))
    ]


def roll(value, shift):
    return pltpu.roll(value, shift % LANES, 1)


def features(centres, segments):
    rows = []
    for c in centres:
        high, middle, low = (part.astype(F32) for part in three_parts(c))
        rows += [high, middle, high, low, high, middle]
    square = centres[0] * centres[0] + centres[1] * centres[1] + centres[2] * centres[2]
    rows += [part.astype(F32) for part in three_parts(square)]
    rows += [jnp.ones_like(square)] * 3
    s, c = segments, centres
    six = [s[0], s[1], s[2]]
    six += [s[1] * c[2] - s[2] * c[1], s[2] * c[0] - s[0] * c[2], s[0] * c[1] - s[1] * c[0]]
    pairs = [two_parts(value) for value in six]
    return rows, [pair[0].astype(F32) for pair in pairs], [pair[1].astype(F32) for pair in pairs]


def step_kernel(
    n_row, n_col, scale, pos_ref, links_ref, panel_ref, smooth_ref, vel_ref,
    grid_ref, part_ref, tgt_ref, send_ref, arrived_ref, b_ref, f_ref, a_ref, acc_ref,
    pair_ref, sum_ref, row_in, total, col_in, row_sum, row_total, col_sum,
    held_ref, out_sem, send_sem, recv_sem, s1, r1, s2, r2, s3, r3, s4, r4, s5, r5,
):
    me_r = lax.axis_index("row")
    me_c = lax.axis_index("col")
    me = me_r * n_col + me_c
    n = n_row * n_col
    slots = pos_ref.shape[1]
    held = 2 * n
    moves = [(y, z, k) for y in range(n_col // 4) for z in range(2) for k in range(2)][1:]
    moves.sort(key=lambda m: -(min(m[0], n_col // 4 - m[0]) + 2 * m[1]))
    far_first = [
        4 * lax.rem(me_c // 4 + y, n_col // 4)
        + 2 * lax.rem(me_c // 2 + z, 2)
        + lax.rem(me_c + k, 2)
        for y, z, k in moves
    ]

    barrier = pltpu.get_barrier_semaphore()
    for step in range(1, n_row):
        to = lax.rem(me_r + step, n_row)
        pl.semaphore_signal(barrier, inc=1, device_id=(to, me_c), device_id_type=MESH)
    for step in range(1, n_col):
        to = lax.rem(me_c + step, n_col)
        pl.semaphore_signal(barrier, inc=1, device_id=(me_r, to), device_id_type=MESH)

    def send_row(source, target, send, recv, steps=tuple(range(1, n_row))):
        copies = []
        for step in steps:
            to = lax.rem(me_r + step, n_row)
            copy = pltpu.make_async_remote_copy(
                src_ref=source(to),
                dst_ref=target(me_r),
                send_sem=send.at[step],
                recv_sem=recv.at[me_r],
                device_id=(to, me_c),
                device_id_type=MESH,
            )
            copy.start()
            copies.append(copy)
        return copies

    def send_col(source, target, send, recv):
        copies = []
        for step, to in enumerate(far_first):
            copy = pltpu.make_async_remote_copy(
                src_ref=source,
                dst_ref=target(me_c),
                send_sem=send.at[step],
                recv_sem=recv.at[me_c],
                device_id=(me_r, to),
                device_id_type=MESH,
            )
            copy.start()
            copies.append(copy)
        return copies

    def wait_from(mine, count, target, recv, steps=None):
        for step in steps or range(1, count):
            frm = lax.rem(mine + step, count)
            pltpu.make_async_copy(target(frm), target(frm), recv.at[frm]).wait()

    def add_up(ref, count):
        value = ref[0]
        for r in range(1, count):
            value = value + ref[r]
        return value

    eye = iota((slots, LANES), 0) == iota((slots, LANES), 1)
    here = pl.ds(pl.multiple_of(me * slots, LANES), LANES)
    owner_row = links_ref[0:1, here].astype(F32)
    follow_row = links_ref[1:2, here].astype(F32)
    follow_col = to_column(follow_row, eye)
    mine_col = (me * slots + iota((slots, 1), 0)).astype(F32)
    lane_row = iota((1, LANES), 1).astype(F32)

    def look(turn, found):
        at = pl.multiple_of(turn * LANES, LANES)
        row = links_ref[1:2, pl.ds(at, LANES)].astype(F32)
        grid_ref[1, pl.ds(turn, 1), :] = row
        grid_ref[0, pl.ds(turn, 1), :] = links_ref[0:1, pl.ds(at, LANES)].astype(F32)
        number = lane_row + (turn * LANES).astype(F32)
        return found + jnp.where(row == mine_col, number, 0.0)

    precede_col = jnp.sum(
        lax.fori_loop(0, n, look, jnp.zeros((slots, LANES), F32), unroll=8),
        axis=1,
        keepdims=True,
    )
    raw = [pos_ref[c] for c in range(3)]
    lane = iota((slots, LANES), 1)
    inside, wraps = [], []
    for x in raw:
        b1, b2, a1, a2 = roll(x, 1), roll(x, 2), roll(x, -1), roll(x, -2)
        zero = jnp.zeros_like(x)
        wrap = (
            4.0 * (jnp.where(lane < 1, b1, zero) + jnp.where(lane > LANES - 2, a1, zero))
            + (jnp.where(lane < 2, b2, zero) + jnp.where(lane > LANES - 3, a2, zero))
        )
        within = (
            6.0 * x
            + 4.0 * (jnp.where(lane < 1, zero, b1) + jnp.where(lane > LANES - 2, zero, a1))
            + (jnp.where(lane < 2, zero, b2) + jnp.where(lane > LANES - 3, zero, a2))
        )
        inside.append(within * 0.0625)
        wraps.append(wrap * 0.0625)
    parts = jnp.concatenate(three_parts(jnp.concatenate(inside, axis=0)), axis=0)
    high = 3 * slots
    edges = pick_lanes((LANES - 2, LANES - 1, 0, 1), wraps)
    edge_parts = jnp.concatenate([part for edge in edges for part in three_parts(edge)], axis=0)
    panel = panel_ref.shape[1]
    part_ref[...] = jnp.zeros_like(part_ref)
    kind = iota((8, panel), 0)
    edge_point = jnp.where(kind < 2, kind + (LANES - 2), jnp.where(kind < 4, kind - 2, -1))
    for r in range(panel_ref.shape[0]):
        flat = panel_ref[r : r + 1, :]
        block = (flat // LANES).astype(F32)
        point = flat % LANES
        one_point = (iota((LANES, panel), 0) == point).astype(BF16)
        got = jnp.dot(parts, one_point, preferred_element_type=F32)
        got = got[:high] + got[high : 2 * high] + got[2 * high :]
        here_mask = block == mine_col
        over = jnp.dot(
            edge_parts, (precede_col == block).astype(BF16), preferred_element_type=F32
        )
        under = jnp.dot(
            edge_parts, (follow_col == block).astype(BF16), preferred_element_type=F32
        )
        beyond = jnp.where(lax.rem(iota(over.shape, 0), 8) < 2, over, under)
        for c in range(3):
            inner = jnp.where(here_mask, got[c * slots : (c + 1) * slots], 0.0)
            outer = beyond[24 * c : 24 * c + 8]
            outer = outer + beyond[24 * c + 8 : 24 * c + 16] + beyond[24 * c + 16 : 24 * c + 24]
            value = jnp.sum(inner, axis=0, keepdims=True) + jnp.sum(
                jnp.where(edge_point == point, outer, 0.0), axis=0, keepdims=True
            )
            for h in range(2):
                part_ref[2 * c + h : 2 * c + h + 1, r * LANES : (r + 1) * LANES] = value[
                    :, h * LANES : (h + 1) * LANES
                ]

    width = LANES

    def lanes(r, size):
        return pl.ds(pl.multiple_of(r * size, size), size)

    def piece(ref, r, size):
        return ref.at[:, lanes(r, size)]

    pl.semaphore_wait(barrier, n_row + n_col - 2)
    copies = send_row(lambda to: piece(part_ref, to, width), lambda r: row_in.at[r], s1, r1)
    row_in[me_r] = part_ref[:, pl.ds(pl.multiple_of(me_r * width, width), width)]

    owner_col = to_column(owner_row, eye)
    earlier = iota((slots, LANES), 0) < iota((slots, LANES), 1)
    same = jnp.logical_and(owner_col == owner_row, earlier)
    rank_row = jnp.sum(jnp.where(same, 1.0, 0.0), axis=0, keepdims=True)
    send_ref[...] = jnp.zeros_like(send_ref)
    to_owner = iota((n, LANES), 0).astype(F32) == owner_row
    for k in range(2):
        chooser = jnp.logical_and(to_owner, rank_row == float(k)).astype(BF16)
        for c, moved in enumerate(pick_rows(chooser, raw)):
            send_ref[pl.ds(2 * c + k, n, stride=8), :] = moved

    wait_from(me_r, n_row, lambda r: row_in.at[r], r1)
    value = add_up(row_in, n_row)
    total[...] = value
    copies += send_col(total, lambda c: col_in.at[c], s2, r2)
    col_in[me_c] = value

    b_ref[...] = jnp.zeros_like(b_ref)
    f_ref[...] = jnp.zeros_like(f_ref)
    inner = jnp.logical_and(lane >= 2, lane < LANES - 3)
    centres, segments = [], []
    for x in raw:
        sm = (6.0 * x + 4.0 * (roll(x, 1) + roll(x, -1)) + (roll(x, 2) + roll(x, -2))) * 0.0625
        ahead = roll(sm, -1)
        segments.append(jnp.where(inner, ahead - sm, 0.0))
        centres.append(0.5 * (ahead + sm))
    rows, highs, lows = features(centres, segments)
    for k, row in enumerate(rows):
        b_ref[pl.ds(k, slots, stride=32), :] = row
    for k in range(6):
        f_ref[pl.ds(k, slots, stride=16), :] = highs[k]
        f_ref[pl.ds(8 + k, slots, stride=16), :] = lows[k]

    wait_from(me_c, n_col, lambda c: col_in.at[c], r2)
    value = add_up(col_in, n_col)
    tgt_ref[:, pl.ds(pl.multiple_of(me_r * width, width), width)] = value
    copies += send_row(
        lambda to: piece(tgt_ref, me_r, width), lambda r: piece(tgt_ref, r, width), s3, r3
    )

    number = (iota((n, LANES), 0) * LANES + iota((n, LANES), 1)).astype(F32)
    mine = grid_ref[0] == me.astype(F32)
    before = (iota((LANES, LANES), 0) < iota((LANES, LANES), 1)).astype(BF16)
    rank = jnp.dot(mine.astype(BF16), before, preferred_element_type=F32)
    ids, nexts, id_rows, next_rows = [], [], [], []
    for k in range(2):
        chosen = jnp.logical_and(mine, rank == float(k))
        count = jnp.sum(jnp.where(chosen, 1.0, 0.0), axis=1, keepdims=True)
        one = jnp.sum(jnp.where(chosen, number, 0.0), axis=1, keepdims=True)
        two = jnp.sum(jnp.where(chosen, grid_ref[1], 0.0), axis=1, keepdims=True)
        ids.append(jnp.where(count > 0.5, one, -1.0))
        nexts.append(jnp.where(count > 0.5, two, -2.0))
        id_rows.append(to_row(ids[k], eye))
        next_rows.append(to_row(nexts[k], eye))
    for k in range(2):
        for m in range(2):
            at = (slice(k * n, (k + 1) * n), slice(m * n, (m + 1) * n))
            pair_ref[0, at[0], at[1]] = jnp.where(nexts[k] == id_rows[m], 1.0, 0.0)
            pair_ref[1, at[0], at[1]] = jnp.where(ids[k] == next_rows[m], 1.0, 0.0)

    def aim(r):
        value = tgt_ref[:, lanes(r, LANES)]
        top, middle, low = (part.astype(F32) for part in three_parts(-2.0 * value))
        square = value * value
        for h in range(2):
            at = pl.ds(pl.multiple_of(r * panel + h * LANES, LANES), LANES)
            k = 0
            for c in range(3):
                for part in (top, top, middle, top, low, middle):
                    a_ref[k : k + 1, at] = part[2 * c + h : 2 * c + h + 1]
                    k += 1
            a_ref[k : k + 3, at] = jnp.ones((3, LANES), F32)
            total_square = square[h : h + 1] + square[2 + h : 3 + h] + square[4 + h : 5 + h]
            for m, part in enumerate(three_parts(total_square + CORE_SQUARED)):
                a_ref[k + 3 + m : k + 4 + m, at] = part.astype(F32)

    def add_blocks(first, count, panels):
        b_at = pl.multiple_of(first * 32, 32)
        f_at = pl.multiple_of(first * 16, 16)
        b = jnp.concatenate(
            [b_ref[pl.ds(b_at + 32 * j, 32), :].astype(BF16) for j in range(count)], axis=1
        )
        f = jnp.concatenate(
            [f_ref[pl.ds(f_at + 16 * j, 16), :].astype(BF16) for j in range(count)], axis=1
        )
        for r in panels:
            at = lanes(r, panel)
            a = a_ref[:, at].astype(BF16)
            q = lax.dot_general(b, a, (((0,), (0,)), ((), ())), preferred_element_type=F32)
            root = lax.rsqrt(q)
            top, low = two_parts(root * root * root)
            acc_ref[:, at] += jnp.dot(f, top, preferred_element_type=F32) + jnp.dot(
                f, low, preferred_element_type=F32
            )

    def velocity_of(r):
        value = tgt_ref[:, lanes(r, LANES)]
        for h in range(2):
            at = pl.ds(pl.multiple_of(r * panel + h * LANES, LANES), LANES)
            t = [value[2 * c + h : 2 * c + h + 1] for c in range(3)]
            s = [acc_ref[k : k + 1, at] + acc_ref[8 + k : 9 + k, at] for k in range(6)]
            v = [
                scale * (s[1] * t[2] - s[2] * t[1] - s[3]),
                scale * (s[2] * t[0] - s[0] * t[2] - s[4]),
                scale * (s[0] * t[1] - s[1] * t[0] - s[5]),
            ]
            for c in range(3):
                sum_ref[2 * c + h : 2 * c + h + 1, lanes(r, LANES)] = v[c]

    near = n_row // 2
    far = [k for k in range(1, n_row) if k != near]
    others = [lax.rem(me_r + k, n_row) for k in far]
    near_r = lax.rem(me_r + near, n_row)
    acc_ref[...] = jnp.zeros_like(acc_ref)
    sum_ref[...] = jnp.zeros_like(sum_ref)
    a_ref[...] = jnp.zeros_like(a_ref)
    aim(me_r)
    for first in range(0, slots // 2, CHUNK // 2):
        add_blocks(first, CHUNK // 2, [me_r])
    wait_from(me_r, n_row, lambda r: piece(tgt_ref, r, width), r3, [near])
    aim(near_r)
    for first in range(0, slots // 2, CHUNK // 2):
        add_blocks(first, CHUNK // 2, [near_r])
    wait_from(me_r, n_row, lambda r: piece(tgt_ref, r, width), r3, far)
    for copy in copies:
        copy.wait_send()
    for r in others:
        aim(r)

    def tile(ref, device):
        return ref.at[pl.ds(pl.multiple_of(device * 8, 8), 8), :]

    def start_block(step):
        to = lax.rem(me + step, n)
        pltpu.make_async_remote_copy(
            src_ref=tile(send_ref, to),
            dst_ref=tile(arrived_ref, me),
            send_sem=send_sem,
            recv_sem=recv_sem,
            device_id=(to // n_col, lax.rem(to, n_col)),
            device_id_type=MESH,
        ).start()

    turns = slots // CHUNK
    each = (n - 1) // turns
    own = pl.ds(pl.multiple_of(me * 8, 8), 8)
    arrived_ref[own, :] = send_ref[own, :]
    for step in range(each * turns + 1, n):
        start_block(step)

    def chunk(turn, carry):
        for j in range(each):
            start_block(turn * each + (j + 1))
        add_blocks(turn * CHUNK, CHUNK, others)
        return carry

    lax.fori_loop(0, turns, chunk, 0)

    rest = pl.ds(0, 8 * (n - 1))
    pltpu.make_async_copy(arrived_ref.at[rest], arrived_ref.at[rest], recv_sem).wait()
    pltpu.make_async_copy(send_ref.at[rest], send_ref.at[rest], send_sem).wait()

    y = [
        jnp.concatenate(
            [arrived_ref[pl.ds(2 * c + k, n, stride=8), :] for k in range(2)], axis=0
        )
        for c in range(3)
    ]
    nxt = pick_rows(pair_ref[0].astype(BF16), y)
    prv = pick_rows(pair_ref[1].astype(BF16), y)
    lane = iota((held, LANES), 1)
    arrays = []
    for c in range(3):
        v, nx, pv = y[c], nxt[c], prv[c]
        a1 = jnp.where(lane < LANES - 1, roll(v, -1), roll(nx, -1))
        a2 = jnp.where(lane < LANES - 2, roll(v, -2), roll(nx, -2))
        b1 = jnp.where(lane < 1, roll(pv, 1), roll(v, 1))
        b2 = jnp.where(lane < 2, roll(pv, 2), roll(v, 2))
        sm = (6.0 * v + 4.0 * (a1 + b1) + (a2 + b2)) * 0.0625
        for k in range(2):
            held_ref[c, pl.ds(k, n, stride=2), :] = sm[k * n : (k + 1) * n]
        after = (
            6.0 * roll(nx, -1) + 4.0 * (roll(nx, -2) + v) + (roll(nx, -3) + roll(v, 1))
        ) * 0.0625
        ahead = jnp.where(lane < LANES - 1, roll(sm, -1), after)
        arrays += [0.5 * (ahead + sm), ahead - sm]
    got = pick_lanes(EDGE_LANES, arrays)
    written = pltpu.make_async_copy(held_ref, smooth_ref, out_sem)
    written.start()
    rows, highs, lows = features(got[0::2], got[1::2])
    for k in range(2):
        at = slice(k * n, (k + 1) * n)
        for m, row in enumerate(rows):
            b_ref[pl.ds((slots + k) * 32 + m, 8, stride=64), :] = row[:, at]
        for m in range(6):
            f_ref[pl.ds((slots + k) * 16 + m, 8, stride=32), :] = highs[m][:, at]
            f_ref[pl.ds((slots + k) * 16 + 8 + m, 8, stride=32), :] = lows[m][:, at]
    add_blocks(slots, 2 * len(EDGE_LANES), others)

    for r in others:
        velocity_of(r)
    for_row = (lambda to: piece(sum_ref, to, LANES), lambda r: row_sum.at[r], s4, r4)
    copies = send_row(*for_row, far)
    for first in range(slots // 2, slots, CHUNK // 2):
        add_blocks(first, CHUNK // 2, [near_r])
    add_blocks(slots, 2 * len(EDGE_LANES), [near_r])
    velocity_of(near_r)
    copies += send_row(*for_row, [near])
    for first in range(slots // 2, slots, CHUNK // 2):
        add_blocks(first, CHUNK // 2, [me_r])
    add_blocks(slots, 2 * len(EDGE_LANES), [me_r])
    velocity_of(me_r)
    row_sum[me_r] = sum_ref[:, pl.ds(pl.multiple_of(me_r * LANES, LANES), LANES)]
    wait_from(me_r, n_row, lambda r: row_sum.at[r], r4)
    value = add_up(row_sum, n_row)
    row_total[...] = value
    copies += send_col(row_total, lambda c: col_sum.at[c], s5, r5)
    col_sum[me_c] = value
    wait_from(me_c, n_col, lambda c: col_sum.at[c], r5)
    value = add_up(col_sum, n_col)
    share = vel_ref.shape[2]
    per_row = LANES // share
    first = lax.rem(me_c, per_row) * share
    pick = (iota((LANES, share), 0) == first + iota((LANES, share), 1)).astype(BF16)
    got = [jnp.dot(part, pick, preferred_element_type=F32) for part in three_parts(value)]
    got = got[0] + got[1] + got[2]
    lower = (iota((1, share), 1) + me_c) < iota((1, share), 1) + per_row
    for c in range(3):
        vel_ref[c] = jnp.where(lower, got[2 * c : 2 * c + 1], got[2 * c + 1 : 2 * c + 2])
    for copy in copies:
        copy.wait_send()
    written.wait()


def shards(n_row, n_col, positions, block_links, panel_points):
    devices = n_row * n_col
    slots, block_len = positions.shape[1:]
    held = 2 * devices
    blocks = block_links.shape[1]
    groups, panel = panel_points.shape
    targets = groups * panel
    width = LANES
    stored = slots + 2 * 8
    scale = 1.0 / (math.pi * math.sqrt(blocks * block_len))
    whole = pl.BlockSpec(memory_space=pltpu.VMEM)
    dma = pltpu.SemaphoreType.DMA
    smoothed, velocity = pl.pallas_call(
        functools.partial(step_kernel, n_row, n_col, scale),
        out_shape=(
            jax.ShapeDtypeStruct((3, held, block_len), F32),
            jax.ShapeDtypeStruct((3, 1, panel // n_col), F32),
        ),
        in_specs=[whole, whole, whole],
        out_specs=(pl.BlockSpec(memory_space=pl.ANY), whole),
        scratch_shapes=[
            pltpu.VMEM((2, devices, slots), F32),
            pltpu.VMEM((8, groups * LANES), F32),
            pltpu.VMEM((8, groups * LANES), F32),
            pltpu.VMEM((8 * devices, block_len), F32),
            pltpu.VMEM((8 * devices, block_len), F32),
            pltpu.VMEM((stored * 32, LANES), F32),
            pltpu.VMEM((stored * 16, LANES), F32),
            pltpu.VMEM((32, targets), F32),
            pltpu.VMEM((16, targets), F32),
            pltpu.VMEM((2, held, held), F32),
            pltpu.VMEM((8, groups * LANES), F32),
            pltpu.VMEM((n_row, 8, width), F32),
            pltpu.VMEM((8, width), F32),
            pltpu.VMEM((n_col, 8, width), F32),
            pltpu.VMEM((n_row, 8, LANES), F32),
            pltpu.VMEM((8, LANES), F32),
            pltpu.VMEM((n_col, 8, LANES), F32),
            pltpu.VMEM((3, held, block_len), F32),
            dma, dma, dma,
            dma((n_row,)), dma((n_row,)),
            dma((n_col,)), dma((n_col,)),
            dma((n_row,)), dma((n_row,)),
            dma((n_row,)), dma((n_row,)),
            dma((n_col,)), dma((n_col,)),
        ],
        compiler_params=pltpu.CompilerParams(
            vmem_limit_bytes=VMEM_LIMIT, collective_id=0, has_side_effects=True
        ),
        name="step",
    )(positions, block_links, panel_points)
    return smoothed, jnp.transpose(velocity, (1, 0, 2))


def solution(mesh):
    placed = (P(None, ("row", "col"), None), P(), P())
    return jax.shard_map(
        functools.partial(shards, mesh.shape["row"], mesh.shape["col"]),
        mesh=mesh,
        in_specs=placed,
        out_specs=(P(None, ("row", "col"), None), P("row", None, "col")),
        check_vma=False,
    )
```

```python
import functools
import math

import jax
import jax.numpy as jnp
from jax import lax
from jax.experimental import pallas as pl
from jax.experimental.pallas import tpu as pltpu
from jax.sharding import PartitionSpec as P

CORE_SQUARED = 0.01
F32 = jnp.float32
BF16 = jnp.bfloat16
LANES = 128
VMEM_LIMIT = 56 << 20
MESH = pl.DeviceIdType.MESH
CHUNK = 32
PART = 8
SMALL = 8
EDGE_LANES = (125, 126, 127, 0, 1)


def iota(shape, axis):
    return lax.broadcasted_iota(jnp.int32, shape, axis)


def three_parts(value):
    high = value.astype(BF16)
    rest = value - high.astype(F32)
    middle = rest.astype(BF16)
    return high, middle, (rest - middle.astype(F32)).astype(BF16)


def two_parts(value):
    high = value.astype(BF16)
    return high, (value - high.astype(F32)).astype(BF16)


def to_column(row, eye):
    return jnp.sum(jnp.where(eye, row, 0.0), axis=1, keepdims=True)


def to_row(column, eye):
    return jnp.sum(jnp.where(eye, column, 0.0), axis=0, keepdims=True)


def pick_rows(chooser, arrays):
    width = arrays[0].shape[1]
    parts = jnp.concatenate([part for array in arrays for part in three_parts(array)], axis=1)
    got = jnp.dot(chooser, parts, preferred_element_type=F32)
    result = []
    for n in range(len(arrays)):
        at = 3 * n * width
        result.append(
            got[:, at : at + width]
            + got[:, at + width : at + 2 * width]
            + got[:, at + 2 * width : at + 3 * width]
        )
    return result


def pick_lanes(lanes, arrays):
    rows = arrays[0].shape[0]
    pick = jnp.zeros((8, LANES), F32)
    for j, where in enumerate(lanes):
        hit = jnp.logical_and(iota((8, LANES), 0) == j, iota((8, LANES), 1) == where)
        pick = pick + jnp.where(hit, 1.0, 0.0)
    stack = jnp.concatenate([part for array in arrays for part in three_parts(array)], axis=0)
    got = lax.dot_general(
        pick.astype(BF16), stack, (((1,), (1,)), ((), ())), preferred_element_type=F32
    )
    return [
        got[:, 3 * m * rows : (3 * m + 1) * rows]
        + got[:, (3 * m + 1) * rows : (3 * m + 2) * rows]
        + got[:, (3 * m + 2) * rows : (3 * m + 3) * rows]
        for m in range(len(arrays))
    ]


def roll(value, shift):
    return pltpu.roll(value, shift % LANES, 1)


def features(centres, segments):
    rows = []
    for c in centres:
        high, middle, low = (part.astype(F32) for part in three_parts(c))
        rows += [high, middle, high, low, high, middle]
    square = centres[0] * centres[0] + centres[1] * centres[1] + centres[2] * centres[2]
    rows += [part.astype(F32) for part in three_parts(square)]
    rows += [jnp.ones_like(square)] * 3
    s, c = segments, centres
    six = [s[0], s[1], s[2]]
    six += [s[1] * c[2] - s[2] * c[1], s[2] * c[0] - s[0] * c[2], s[0] * c[1] - s[1] * c[0]]
    pairs = [two_parts(value) for value in six]
    return rows, [pair[0].astype(F32) for pair in pairs], [pair[1].astype(F32) for pair in pairs]


def step_kernel(
    n_row, n_col, scale, pos_ref, links_ref, panel_ref, smooth_ref, vel_ref,
    grid_ref, part_ref, tgt_ref, send_ref, arrived_ref, b_ref, f_ref, a_ref, acc_ref,
    pair_ref, sum_ref, row_in, total, col_in, row_sum, row_total, col_sum,
    held_ref, out_sem, send_sem, recv_sem, s1, r1, s2, r2, s3, r3, s4, r4, s5, r5,
):
    me_r = lax.axis_index("row")
    me_c = lax.axis_index("col")
    me = me_r * n_col + me_c
    n = n_row * n_col
    slots = pos_ref.shape[1]
    held = 2 * n
    moves = [(y, z, k) for y in range(n_col // 4) for z in range(2) for k in range(2)][1:]
    moves.sort(key=lambda m: -(min(m[0], n_col // 4 - m[0]) + 2 * m[1]))
    far_first = [
        4 * lax.rem(me_c // 4 + y, n_col // 4)
        + 2 * lax.rem(me_c // 2 + z, 2)
        + lax.rem(me_c + k, 2)
        for y, z, k in moves
    ]

    barrier = pltpu.get_barrier_semaphore()
    for step in range(1, n_row):
        to = lax.rem(me_r + step, n_row)
        pl.semaphore_signal(barrier, inc=1, device_id=(to, me_c), device_id_type=MESH)
    for step in range(1, n_col):
        to = lax.rem(me_c + step, n_col)
        pl.semaphore_signal(barrier, inc=1, device_id=(me_r, to), device_id_type=MESH)

    def send_row(source, target, send, recv, steps=tuple(range(1, n_row))):
        copies = []
        for step in steps:
            to = lax.rem(me_r + step, n_row)
            copy = pltpu.make_async_remote_copy(
                src_ref=source(to),
                dst_ref=target(me_r),
                send_sem=send.at[step],
                recv_sem=recv.at[me_r],
                device_id=(to, me_c),
                device_id_type=MESH,
            )
            copy.start()
            copies.append(copy)
        return copies

    def send_col(source, target, send, recv):
        copies = []
        for step, to in enumerate(far_first):
            copy = pltpu.make_async_remote_copy(
                src_ref=source,
                dst_ref=target(me_c),
                send_sem=send.at[step],
                recv_sem=recv.at[me_c],
                device_id=(me_r, to),
                device_id_type=MESH,
            )
            copy.start()
            copies.append(copy)
        return copies

    def wait_from(mine, count, target, recv, steps=None):
        for step in steps or range(1, count):
            frm = lax.rem(mine + step, count)
            pltpu.make_async_copy(target(frm), target(frm), recv.at[frm]).wait()

    def add_up(ref, count):
        value = ref[0]
        for r in range(1, count):
            value = value + ref[r]
        return value

    eye = iota((slots, LANES), 0) == iota((slots, LANES), 1)
    here = pl.ds(pl.multiple_of(me * slots, LANES), LANES)
    owner_row = links_ref[0:1, here].astype(F32)
    follow_row = links_ref[1:2, here].astype(F32)
    follow_col = to_column(follow_row, eye)
    mine_col = (me * slots + iota((slots, 1), 0)).astype(F32)
    lane_row = iota((1, LANES), 1).astype(F32)

    def look(turn, found):
        at = pl.multiple_of(turn * LANES, LANES)
        row = links_ref[1:2, pl.ds(at, LANES)].astype(F32)
        grid_ref[1, pl.ds(turn, 1), :] = row
        grid_ref[0, pl.ds(turn, 1), :] = links_ref[0:1, pl.ds(at, LANES)].astype(F32)
        number = lane_row + (turn * LANES).astype(F32)
        return found + jnp.where(row == mine_col, number, 0.0)

    precede_col = jnp.sum(
        lax.fori_loop(0, n, look, jnp.zeros((slots, LANES), F32), unroll=8),
        axis=1,
        keepdims=True,
    )
    raw = [pos_ref[c] for c in range(3)]
    lane = iota((slots, LANES), 1)
    inside, wraps = [], []
    for x in raw:
        b1, b2, a1, a2 = roll(x, 1), roll(x, 2), roll(x, -1), roll(x, -2)
        zero = jnp.zeros_like(x)
        wrap = (
            4.0 * (jnp.where(lane < 1, b1, zero) + jnp.where(lane > LANES - 2, a1, zero))
            + (jnp.where(lane < 2, b2, zero) + jnp.where(lane > LANES - 3, a2, zero))
        )
        within = (
            6.0 * x
            + 4.0 * (jnp.where(lane < 1, zero, b1) + jnp.where(lane > LANES - 2, zero, a1))
            + (jnp.where(lane < 2, zero, b2) + jnp.where(lane > LANES - 3, zero, a2))
        )
        inside.append(within * 0.0625)
        wraps.append(wrap * 0.0625)
    parts = jnp.concatenate(three_parts(jnp.concatenate(inside, axis=0)), axis=0)
    high = 3 * slots
    edges = pick_lanes((LANES - 2, LANES - 1, 0, 1), wraps)
    edge_parts = jnp.concatenate([part for edge in edges for part in three_parts(edge)], axis=0)
    panel = panel_ref.shape[1]
    part_ref[...] = jnp.zeros_like(part_ref)
    kind = iota((8, panel), 0)
    edge_point = jnp.where(kind < 2, kind + (LANES - 2), jnp.where(kind < 4, kind - 2, -1))
    for r in range(panel_ref.shape[0]):
        flat = panel_ref[r : r + 1, :]
        block = (flat // LANES).astype(F32)
        point = flat % LANES
        one_point = (iota((LANES, panel), 0) == point).astype(BF16)
        got = jnp.dot(parts, one_point, preferred_element_type=F32)
        got = got[:high] + got[high : 2 * high] + got[2 * high :]
        here_mask = block == mine_col
        over = jnp.dot(
            edge_parts, (precede_col == block).astype(BF16), preferred_element_type=F32
        )
        under = jnp.dot(
            edge_parts, (follow_col == block).astype(BF16), preferred_element_type=F32
        )
        beyond = jnp.where(lax.rem(iota(over.shape, 0), 8) < 2, over, under)
        for c in range(3):
            inner = jnp.where(here_mask, got[c * slots : (c + 1) * slots], 0.0)
            outer = beyond[24 * c : 24 * c + 8]
            outer = outer + beyond[24 * c + 8 : 24 * c + 16] + beyond[24 * c + 16 : 24 * c + 24]
            value = jnp.sum(inner, axis=0, keepdims=True) + jnp.sum(
                jnp.where(edge_point == point, outer, 0.0), axis=0, keepdims=True
            )
            for h in range(2):
                part_ref[2 * c + h : 2 * c + h + 1, r * LANES : (r + 1) * LANES] = value[
                    :, h * LANES : (h + 1) * LANES
                ]

    width = LANES

    def lanes(r, size):
        return pl.ds(pl.multiple_of(r * size, size), size)

    def piece(ref, r, size):
        return ref.at[:, lanes(r, size)]

    pl.semaphore_wait(barrier, n_row + n_col - 2)
    copies = send_row(lambda to: piece(part_ref, to, width), lambda r: row_in.at[r], s1, r1)
    row_in[me_r] = part_ref[:, pl.ds(pl.multiple_of(me_r * width, width), width)]

    owner_col = to_column(owner_row, eye)
    earlier = iota((slots, LANES), 0) < iota((slots, LANES), 1)
    same = jnp.logical_and(owner_col == owner_row, earlier)
    rank_row = jnp.sum(jnp.where(same, 1.0, 0.0), axis=0, keepdims=True)
    send_ref[...] = jnp.zeros_like(send_ref)
    to_owner = iota((n, LANES), 0).astype(F32) == owner_row
    for k in range(2):
        chooser = jnp.logical_and(to_owner, rank_row == float(k)).astype(BF16)
        for c, moved in enumerate(pick_rows(chooser, raw)):
            send_ref[pl.ds(2 * c + k, n, stride=8), :] = moved

    wait_from(me_r, n_row, lambda r: row_in.at[r], r1)
    value = add_up(row_in, n_row)
    total[...] = value
    copies += send_col(total, lambda c: col_in.at[c], s2, r2)
    col_in[me_c] = value

    b_ref[...] = jnp.zeros_like(b_ref)
    f_ref[...] = jnp.zeros_like(f_ref)
    inner = jnp.logical_and(lane >= 2, lane < LANES - 3)
    centres, segments = [], []
    for x in raw:
        sm = (6.0 * x + 4.0 * (roll(x, 1) + roll(x, -1)) + (roll(x, 2) + roll(x, -2))) * 0.0625
        ahead = roll(sm, -1)
        segments.append(jnp.where(inner, ahead - sm, 0.0))
        centres.append(0.5 * (ahead + sm))
    rows, highs, lows = features(centres, segments)
    for k, row in enumerate(rows):
        b_ref[pl.ds(k, slots, stride=32), :] = row
    for k in range(6):
        f_ref[pl.ds(k, slots, stride=16), :] = highs[k]
        f_ref[pl.ds(8 + k, slots, stride=16), :] = lows[k]

    wait_from(me_c, n_col, lambda c: col_in.at[c], r2)
    value = add_up(col_in, n_col)
    tgt_ref[:, pl.ds(pl.multiple_of(me_r * width, width), width)] = value
    copies += send_row(
        lambda to: piece(tgt_ref, me_r, width), lambda r: piece(tgt_ref, r, width), s3, r3
    )

    number = (iota((n, LANES), 0) * LANES + iota((n, LANES), 1)).astype(F32)
    mine = grid_ref[0] == me.astype(F32)
    before = (iota((LANES, LANES), 0) < iota((LANES, LANES), 1)).astype(BF16)
    rank = jnp.dot(mine.astype(BF16), before, preferred_element_type=F32)
    ids, nexts, id_rows, next_rows = [], [], [], []
    for k in range(2):
        chosen = jnp.logical_and(mine, rank == float(k))
        count = jnp.sum(jnp.where(chosen, 1.0, 0.0), axis=1, keepdims=True)
        one = jnp.sum(jnp.where(chosen, number, 0.0), axis=1, keepdims=True)
        two = jnp.sum(jnp.where(chosen, grid_ref[1], 0.0), axis=1, keepdims=True)
        ids.append(jnp.where(count > 0.5, one, -1.0))
        nexts.append(jnp.where(count > 0.5, two, -2.0))
        id_rows.append(to_row(ids[k], eye))
        next_rows.append(to_row(nexts[k], eye))
    for k in range(2):
        for m in range(2):
            at = (slice(k * n, (k + 1) * n), slice(m * n, (m + 1) * n))
            pair_ref[0, at[0], at[1]] = jnp.where(nexts[k] == id_rows[m], 1.0, 0.0)
            pair_ref[1, at[0], at[1]] = jnp.where(ids[k] == next_rows[m], 1.0, 0.0)

    def aim(r):
        value = tgt_ref[:, lanes(r, LANES)]
        top, middle, low = (part.astype(F32) for part in three_parts(-2.0 * value))
        square = value * value
        for h in range(2):
            at = pl.ds(pl.multiple_of(r * panel + h * LANES, LANES), LANES)
            k = 0
            for c in range(3):
                for part in (top, top, middle, top, low, middle):
                    a_ref[k : k + 1, at] = part[2 * c + h : 2 * c + h + 1]
                    k += 1
            a_ref[k : k + 3, at] = jnp.ones((3, LANES), F32)
            total_square = square[h : h + 1] + square[2 + h : 3 + h] + square[4 + h : 5 + h]
            for m, part in enumerate(three_parts(total_square + CORE_SQUARED)):
                a_ref[k + 3 + m : k + 4 + m, at] = part.astype(F32)

    def add_blocks(first, count, panels):
        b_at = pl.multiple_of(first * 32, 32)
        f_at = pl.multiple_of(first * 16, 16)
        b = jnp.concatenate(
            [b_ref[pl.ds(b_at + 32 * j, 32), :].astype(BF16) for j in range(count)], axis=1
        )
        f = jnp.concatenate(
            [f_ref[pl.ds(f_at + 16 * j, 16), :].astype(BF16) for j in range(count)], axis=1
        )
        for r in panels:
            at = lanes(r, panel)
            a = a_ref[:, at].astype(BF16)
            q = lax.dot_general(b, a, (((0,), (0,)), ((), ())), preferred_element_type=F32)
            root = lax.rsqrt(q)
            top, low = two_parts(root * root * root)
            acc_ref[:, at] += jnp.dot(f, top, preferred_element_type=F32) + jnp.dot(
                f, low, preferred_element_type=F32
            )

    def velocity_of(r):
        value = tgt_ref[:, lanes(r, LANES)]
        for h in range(2):
            at = pl.ds(pl.multiple_of(r * panel + h * LANES, LANES), LANES)
            t = [value[2 * c + h : 2 * c + h + 1] for c in range(3)]
            s = [acc_ref[k : k + 1, at] + acc_ref[8 + k : 9 + k, at] for k in range(6)]
            v = [
                scale * (s[1] * t[2] - s[2] * t[1] - s[3]),
                scale * (s[2] * t[0] - s[0] * t[2] - s[4]),
                scale * (s[0] * t[1] - s[1] * t[0] - s[5]),
            ]
            for c in range(3):
                sum_ref[2 * c + h : 2 * c + h + 1, lanes(r, LANES)] = v[c]

    near = n_row // 2
    far = [k for k in range(1, n_row) if k != near]
    others = [lax.rem(me_r + k, n_row) for k in far]
    near_r = lax.rem(me_r + near, n_row)
    acc_ref[...] = jnp.zeros_like(acc_ref)
    sum_ref[...] = jnp.zeros_like(sum_ref)
    a_ref[...] = jnp.zeros_like(a_ref)
    aim(me_r)
    for first in range(0, slots // 2, SMALL):
        add_blocks(first, SMALL, [me_r])
    wait_from(me_r, n_row, lambda r: piece(tgt_ref, r, width), r3, [near])
    aim(near_r)
    for first in range(0, slots // 2, SMALL):
        add_blocks(first, SMALL, [near_r])
    wait_from(me_r, n_row, lambda r: piece(tgt_ref, r, width), r3, far)
    for copy in copies:
        copy.wait_send()
    for r in others:
        aim(r)

    def tile(ref, device):
        return ref.at[pl.ds(pl.multiple_of(device * 8, 8), 8), :]

    def start_block(step):
        to = lax.rem(me + step, n)
        pltpu.make_async_remote_copy(
            src_ref=tile(send_ref, to),
            dst_ref=tile(arrived_ref, me),
            send_sem=send_sem,
            recv_sem=recv_sem,
            device_id=(to // n_col, lax.rem(to, n_col)),
            device_id_type=MESH,
        ).start()

    turns = slots // CHUNK
    each = (n - 1) // turns
    own = pl.ds(pl.multiple_of(me * 8, 8), 8)
    arrived_ref[own, :] = send_ref[own, :]
    for step in range(each * turns + 1, n):
        start_block(step)

    def chunk(turn, carry):
        for j in range(each):
            start_block(turn * each + (j + 1))
        for first in range(0, CHUNK, PART):
            add_blocks(turn * CHUNK + first, PART, others)
        return carry

    lax.fori_loop(0, turns, chunk, 0)

    rest = pl.ds(0, 8 * (n - 1))
    pltpu.make_async_copy(arrived_ref.at[rest], arrived_ref.at[rest], recv_sem).wait()
    pltpu.make_async_copy(send_ref.at[rest], send_ref.at[rest], send_sem).wait()

    y = [
        jnp.concatenate(
            [arrived_ref[pl.ds(2 * c + k, n, stride=8), :] for k in range(2)], axis=0
        )
        for c in range(3)
    ]
    nxt = pick_rows(pair_ref[0].astype(BF16), y)
    prv = pick_rows(pair_ref[1].astype(BF16), y)
    lane = iota((held, LANES), 1)
    arrays = []
    for c in range(3):
        v, nx, pv = y[c], nxt[c], prv[c]
        a1 = jnp.where(lane < LANES - 1, roll(v, -1), roll(nx, -1))
        a2 = jnp.where(lane < LANES - 2, roll(v, -2), roll(nx, -2))
        b1 = jnp.where(lane < 1, roll(pv, 1), roll(v, 1))
        b2 = jnp.where(lane < 2, roll(pv, 2), roll(v, 2))
        sm = (6.0 * v + 4.0 * (a1 + b1) + (a2 + b2)) * 0.0625
        for k in range(2):
            held_ref[c, pl.ds(k, n, stride=2), :] = sm[k * n : (k + 1) * n]
        after = (
            6.0 * roll(nx, -1) + 4.0 * (roll(nx, -2) + v) + (roll(nx, -3) + roll(v, 1))
        ) * 0.0625
        ahead = jnp.where(lane < LANES - 1, roll(sm, -1), after)
        arrays += [0.5 * (ahead + sm), ahead - sm]
    got = pick_lanes(EDGE_LANES, arrays)
    written = pltpu.make_async_copy(held_ref, smooth_ref, out_sem)
    written.start()
    rows, highs, lows = features(got[0::2], got[1::2])
    for k in range(2):
        at = slice(k * n, (k + 1) * n)
        for m, row in enumerate(rows):
            b_ref[pl.ds((slots + k) * 32 + m, 8, stride=64), :] = row[:, at]
        for m in range(6):
            f_ref[pl.ds((slots + k) * 16 + m, 8, stride=32), :] = highs[m][:, at]
            f_ref[pl.ds((slots + k) * 16 + 8 + m, 8, stride=32), :] = lows[m][:, at]
    add_blocks(slots, 2 * len(EDGE_LANES), others)

    for r in others:
        velocity_of(r)
    for_row = (lambda to: piece(sum_ref, to, LANES), lambda r: row_sum.at[r], s4, r4)
    copies = send_row(*for_row, far)
    for first in range(slots // 2, slots, SMALL):
        add_blocks(first, SMALL, [near_r])
    add_blocks(slots, 2 * len(EDGE_LANES), [near_r])
    velocity_of(near_r)
    copies += send_row(*for_row, [near])
    for first in range(slots // 2, slots, SMALL):
        add_blocks(first, SMALL, [me_r])
    add_blocks(slots, 2 * len(EDGE_LANES), [me_r])
    velocity_of(me_r)
    row_sum[me_r] = sum_ref[:, pl.ds(pl.multiple_of(me_r * LANES, LANES), LANES)]
    wait_from(me_r, n_row, lambda r: row_sum.at[r], r4)
    value = add_up(row_sum, n_row)
    row_total[...] = value
    copies += send_col(row_total, lambda c: col_sum.at[c], s5, r5)
    col_sum[me_c] = value
    wait_from(me_c, n_col, lambda c: col_sum.at[c], r5)
    value = add_up(col_sum, n_col)
    share = vel_ref.shape[2]
    per_row = LANES // share
    first = lax.rem(me_c, per_row) * share
    pick = (iota((LANES, share), 0) == first + iota((LANES, share), 1)).astype(BF16)
    got = [jnp.dot(part, pick, preferred_element_type=F32) for part in three_parts(value)]
    got = got[0] + got[1] + got[2]
    lower = (iota((1, share), 1) + me_c) < iota((1, share), 1) + per_row
    for c in range(3):
        vel_ref[c] = jnp.where(lower, got[2 * c : 2 * c + 1], got[2 * c + 1 : 2 * c + 2])
    for copy in copies:
        copy.wait_send()
    written.wait()


def shards(n_row, n_col, positions, block_links, panel_points):
    devices = n_row * n_col
    slots, block_len = positions.shape[1:]
    held = 2 * devices
    blocks = block_links.shape[1]
    groups, panel = panel_points.shape
    targets = groups * panel
    width = LANES
    stored = slots + 2 * 8
    scale = 1.0 / (math.pi * math.sqrt(blocks * block_len))
    whole = pl.BlockSpec(memory_space=pltpu.VMEM)
    dma = pltpu.SemaphoreType.DMA
    smoothed, velocity = pl.pallas_call(
        functools.partial(step_kernel, n_row, n_col, scale),
        out_shape=(
            jax.ShapeDtypeStruct((3, held, block_len), F32),
            jax.ShapeDtypeStruct((3, 1, panel // n_col), F32),
        ),
        in_specs=[whole, whole, whole],
        out_specs=(pl.BlockSpec(memory_space=pl.ANY), whole),
        scratch_shapes=[
            pltpu.VMEM((2, devices, slots), F32),
            pltpu.VMEM((8, groups * LANES), F32),
            pltpu.VMEM((8, groups * LANES), F32),
            pltpu.VMEM((8 * devices, block_len), F32),
            pltpu.VMEM((8 * devices, block_len), F32),
            pltpu.VMEM((stored * 32, LANES), F32),
            pltpu.VMEM((stored * 16, LANES), F32),
            pltpu.VMEM((32, targets), F32),
            pltpu.VMEM((16, targets), F32),
            pltpu.VMEM((2, held, held), F32),
            pltpu.VMEM((8, groups * LANES), F32),
            pltpu.VMEM((n_row, 8, width), F32),
            pltpu.VMEM((8, width), F32),
            pltpu.VMEM((n_col, 8, width), F32),
            pltpu.VMEM((n_row, 8, LANES), F32),
            pltpu.VMEM((8, LANES), F32),
            pltpu.VMEM((n_col, 8, LANES), F32),
            pltpu.VMEM((3, held, block_len), F32),
            dma, dma, dma,
            dma((n_row,)), dma((n_row,)),
            dma((n_col,)), dma((n_col,)),
            dma((n_row,)), dma((n_row,)),
            dma((n_row,)), dma((n_row,)),
            dma((n_col,)), dma((n_col,)),
        ],
        compiler_params=pltpu.CompilerParams(
            vmem_limit_bytes=VMEM_LIMIT, collective_id=0, has_side_effects=True
        ),
        name="step",
    )(positions, block_links, panel_points)
    return smoothed, jnp.transpose(velocity, (1, 0, 2))


def solution(mesh):
    placed = (P(None, ("row", "col"), None), P(), P())
    return jax.shard_map(
        functools.partial(shards, mesh.shape["row"], mesh.shape["col"]),
        mesh=mesh,
        in_specs=placed,
        out_specs=(P(None, ("row", "col"), None), P("row", None, "col")),
        check_vma=False,
    )
```

```python
import functools
import math

import jax
import jax.numpy as jnp
from jax import lax
from jax.experimental import pallas as pl
from jax.experimental.pallas import tpu as pltpu
from jax.sharding import PartitionSpec as P

CORE_SQUARED = 0.01
F32 = jnp.float32
BF16 = jnp.bfloat16
LANES = 128
VMEM_LIMIT = 56 << 20
MESH = pl.DeviceIdType.MESH
CHUNK = 32
PART = 4
SMALL = 8
EDGE_LANES = (125, 126, 127, 0, 1)


def iota(shape, axis):
    return lax.broadcasted_iota(jnp.int32, shape, axis)


def three_parts(value):
    high = value.astype(BF16)
    rest = value - high.astype(F32)
    middle = rest.astype(BF16)
    return high, middle, (rest - middle.astype(F32)).astype(BF16)


def two_parts(value):
    high = value.astype(BF16)
    return high, (value - high.astype(F32)).astype(BF16)


def to_column(row, eye):
    return jnp.sum(jnp.where(eye, row, 0.0), axis=1, keepdims=True)


def to_row(column, eye):
    return jnp.sum(jnp.where(eye, column, 0.0), axis=0, keepdims=True)


def pick_rows(chooser, arrays):
    width = arrays[0].shape[1]
    parts = jnp.concatenate([part for array in arrays for part in three_parts(array)], axis=1)
    got = jnp.dot(chooser, parts, preferred_element_type=F32)
    result = []
    for n in range(len(arrays)):
        at = 3 * n * width
        result.append(
            got[:, at : at + width]
            + got[:, at + width : at + 2 * width]
            + got[:, at + 2 * width : at + 3 * width]
        )
    return result


def pick_lanes(lanes, arrays):
    rows = arrays[0].shape[0]
    pick = jnp.zeros((8, LANES), F32)
    for j, where in enumerate(lanes):
        hit = jnp.logical_and(iota((8, LANES), 0) == j, iota((8, LANES), 1) == where)
        pick = pick + jnp.where(hit, 1.0, 0.0)
    stack = jnp.concatenate([part for array in arrays for part in three_parts(array)], axis=0)
    got = lax.dot_general(
        pick.astype(BF16), stack, (((1,), (1,)), ((), ())), preferred_element_type=F32
    )
    return [
        got[:, 3 * m * rows : (3 * m + 1) * rows]
        + got[:, (3 * m + 1) * rows : (3 * m + 2) * rows]
        + got[:, (3 * m + 2) * rows : (3 * m + 3) * rows]
        for m in range(len(arrays))
    ]


def roll(value, shift):
    return pltpu.roll(value, shift % LANES, 1)


def features(centres, segments):
    rows = []
    for c in centres:
        high, middle, low = (part.astype(F32) for part in three_parts(c))
        rows += [high, middle, high, low, high, middle]
    square = centres[0] * centres[0] + centres[1] * centres[1] + centres[2] * centres[2]
    rows += [part.astype(F32) for part in three_parts(square)]
    rows += [jnp.ones_like(square)] * 3
    s, c = segments, centres
    six = [s[0], s[1], s[2]]
    six += [s[1] * c[2] - s[2] * c[1], s[2] * c[0] - s[0] * c[2], s[0] * c[1] - s[1] * c[0]]
    pairs = [two_parts(value) for value in six]
    return rows, [pair[0].astype(F32) for pair in pairs], [pair[1].astype(F32) for pair in pairs]


def step_kernel(
    n_row, n_col, scale, pos_ref, links_ref, panel_ref, smooth_ref, vel_ref,
    grid_ref, part_ref, tgt_ref, send_ref, arrived_ref, b_ref, f_ref, a_ref, acc_ref,
    pair_ref, sum_ref, row_in, total, col_in, row_sum, row_total, col_sum,
    held_ref, out_sem, send_sem, recv_sem, s1, r1, s2, r2, s3, r3, s4, r4, s5, r5,
):
    me_r = lax.axis_index("row")
    me_c = lax.axis_index("col")
    me = me_r * n_col + me_c
    n = n_row * n_col
    slots = pos_ref.shape[1]
    held = 2 * n
    moves = [(y, z, k) for y in range(n_col // 4) for z in range(2) for k in range(2)][1:]
    moves.sort(key=lambda m: -(min(m[0], n_col // 4 - m[0]) + 2 * m[1]))
    far_first = [
        4 * lax.rem(me_c // 4 + y, n_col // 4)
        + 2 * lax.rem(me_c // 2 + z, 2)
        + lax.rem(me_c + k, 2)
        for y, z, k in moves
    ]

    barrier = pltpu.get_barrier_semaphore()
    for step in range(1, n_row):
        to = lax.rem(me_r + step, n_row)
        pl.semaphore_signal(barrier, inc=1, device_id=(to, me_c), device_id_type=MESH)
    for step in range(1, n_col):
        to = lax.rem(me_c + step, n_col)
        pl.semaphore_signal(barrier, inc=1, device_id=(me_r, to), device_id_type=MESH)

    def send_row(source, target, send, recv, steps=tuple(range(1, n_row))):
        copies = []
        for step in steps:
            to = lax.rem(me_r + step, n_row)
            copy = pltpu.make_async_remote_copy(
                src_ref=source(to),
                dst_ref=target(me_r),
                send_sem=send.at[step],
                recv_sem=recv.at[me_r],
                device_id=(to, me_c),
                device_id_type=MESH,
            )
            copy.start()
            copies.append(copy)
        return copies

    def send_col(source, target, send, recv):
        copies = []
        for step, to in enumerate(far_first):
            copy = pltpu.make_async_remote_copy(
                src_ref=source,
                dst_ref=target(me_c),
                send_sem=send.at[step],
                recv_sem=recv.at[me_c],
                device_id=(me_r, to),
                device_id_type=MESH,
            )
            copy.start()
            copies.append(copy)
        return copies

    def wait_from(mine, count, target, recv, steps=None):
        for step in steps or range(1, count):
            frm = lax.rem(mine + step, count)
            pltpu.make_async_copy(target(frm), target(frm), recv.at[frm]).wait()

    def add_up(ref, count):
        value = ref[0]
        for r in range(1, count):
            value = value + ref[r]
        return value

    eye = iota((slots, LANES), 0) == iota((slots, LANES), 1)
    here = pl.ds(pl.multiple_of(me * slots, LANES), LANES)
    owner_row = links_ref[0:1, here].astype(F32)
    follow_row = links_ref[1:2, here].astype(F32)
    follow_col = to_column(follow_row, eye)
    mine_col = (me * slots + iota((slots, 1), 0)).astype(F32)
    lane_row = iota((1, LANES), 1).astype(F32)

    def look(turn, found):
        at = pl.multiple_of(turn * LANES, LANES)
        row = links_ref[1:2, pl.ds(at, LANES)].astype(F32)
        grid_ref[1, pl.ds(turn, 1), :] = row
        grid_ref[0, pl.ds(turn, 1), :] = links_ref[0:1, pl.ds(at, LANES)].astype(F32)
        number = lane_row + (turn * LANES).astype(F32)
        return found + jnp.where(row == mine_col, number, 0.0)

    precede_col = jnp.sum(
        lax.fori_loop(0, n, look, jnp.zeros((slots, LANES), F32), unroll=8),
        axis=1,
        keepdims=True,
    )
    raw = [pos_ref[c] for c in range(3)]
    lane = iota((slots, LANES), 1)
    inside, wraps = [], []
    for x in raw:
        b1, b2, a1, a2 = roll(x, 1), roll(x, 2), roll(x, -1), roll(x, -2)
        zero = jnp.zeros_like(x)
        wrap = (
            4.0 * (jnp.where(lane < 1, b1, zero) + jnp.where(lane > LANES - 2, a1, zero))
            + (jnp.where(lane < 2, b2, zero) + jnp.where(lane > LANES - 3, a2, zero))
        )
        within = (
            6.0 * x
            + 4.0 * (jnp.where(lane < 1, zero, b1) + jnp.where(lane > LANES - 2, zero, a1))
            + (jnp.where(lane < 2, zero, b2) + jnp.where(lane > LANES - 3, zero, a2))
        )
        inside.append(within * 0.0625)
        wraps.append(wrap * 0.0625)
    parts = jnp.concatenate(three_parts(jnp.concatenate(inside, axis=0)), axis=0)
    high = 3 * slots
    edges = pick_lanes((LANES - 2, LANES - 1, 0, 1), wraps)
    edge_parts = jnp.concatenate([part for edge in edges for part in three_parts(edge)], axis=0)
    panel = panel_ref.shape[1]
    part_ref[...] = jnp.zeros_like(part_ref)
    kind = iota((8, panel), 0)
    edge_point = jnp.where(kind < 2, kind + (LANES - 2), jnp.where(kind < 4, kind - 2, -1))
    for r in range(panel_ref.shape[0]):
        flat = panel_ref[r : r + 1, :]
        block = (flat // LANES).astype(F32)
        point = flat % LANES
        one_point = (iota((LANES, panel), 0) == point).astype(BF16)
        got = jnp.dot(parts, one_point, preferred_element_type=F32)
        got = got[:high] + got[high : 2 * high] + got[2 * high :]
        here_mask = block == mine_col
        over = jnp.dot(
            edge_parts, (precede_col == block).astype(BF16), preferred_element_type=F32
        )
        under = jnp.dot(
            edge_parts, (follow_col == block).astype(BF16), preferred_element_type=F32
        )
        beyond = jnp.where(lax.rem(iota(over.shape, 0), 8) < 2, over, under)
        for c in range(3):
            inner = jnp.where(here_mask, got[c * slots : (c + 1) * slots], 0.0)
            outer = beyond[24 * c : 24 * c + 8]
            outer = outer + beyond[24 * c + 8 : 24 * c + 16] + beyond[24 * c + 16 : 24 * c + 24]
            value = jnp.sum(inner, axis=0, keepdims=True) + jnp.sum(
                jnp.where(edge_point == point, outer, 0.0), axis=0, keepdims=True
            )
            for h in range(2):
                part_ref[2 * c + h : 2 * c + h + 1, r * LANES : (r + 1) * LANES] = value[
                    :, h * LANES : (h + 1) * LANES
                ]

    width = LANES

    def lanes(r, size):
        return pl.ds(pl.multiple_of(r * size, size), size)

    def piece(ref, r, size):
        return ref.at[:, lanes(r, size)]

    pl.semaphore_wait(barrier, n_row + n_col - 2)
    copies = send_row(lambda to: piece(part_ref, to, width), lambda r: row_in.at[r], s1, r1)
    row_in[me_r] = part_ref[:, pl.ds(pl.multiple_of(me_r * width, width), width)]

    owner_col = to_column(owner_row, eye)
    earlier = iota((slots, LANES), 0) < iota((slots, LANES), 1)
    same = jnp.logical_and(owner_col == owner_row, earlier)
    rank_row = jnp.sum(jnp.where(same, 1.0, 0.0), axis=0, keepdims=True)
    send_ref[...] = jnp.zeros_like(send_ref)
    to_owner = iota((n, LANES), 0).astype(F32) == owner_row
    for k in range(2):
        chooser = jnp.logical_and(to_owner, rank_row == float(k)).astype(BF16)
        for c, moved in enumerate(pick_rows(chooser, raw)):
            send_ref[pl.ds(2 * c + k, n, stride=8), :] = moved

    wait_from(me_r, n_row, lambda r: row_in.at[r], r1)
    value = add_up(row_in, n_row)
    total[...] = value
    copies += send_col(total, lambda c: col_in.at[c], s2, r2)
    col_in[me_c] = value

    b_ref[...] = jnp.zeros_like(b_ref)
    f_ref[...] = jnp.zeros_like(f_ref)
    inner = jnp.logical_and(lane >= 2, lane < LANES - 3)
    centres, segments = [], []
    for x in raw:
        sm = (6.0 * x + 4.0 * (roll(x, 1) + roll(x, -1)) + (roll(x, 2) + roll(x, -2))) * 0.0625
        ahead = roll(sm, -1)
        segments.append(jnp.where(inner, ahead - sm, 0.0))
        centres.append(0.5 * (ahead + sm))
    rows, highs, lows = features(centres, segments)
    for k, row in enumerate(rows):
        b_ref[pl.ds(k, slots, stride=32), :] = row
    for k in range(6):
        f_ref[pl.ds(k, slots, stride=16), :] = highs[k]
        f_ref[pl.ds(8 + k, slots, stride=16), :] = lows[k]

    wait_from(me_c, n_col, lambda c: col_in.at[c], r2)
    value = add_up(col_in, n_col)
    tgt_ref[:, pl.ds(pl.multiple_of(me_r * width, width), width)] = value
    copies += send_row(
        lambda to: piece(tgt_ref, me_r, width), lambda r: piece(tgt_ref, r, width), s3, r3
    )

    number = (iota((n, LANES), 0) * LANES + iota((n, LANES), 1)).astype(F32)
    mine = grid_ref[0] == me.astype(F32)
    before = (iota((LANES, LANES), 0) < iota((LANES, LANES), 1)).astype(BF16)
    rank = jnp.dot(mine.astype(BF16), before, preferred_element_type=F32)
    ids, nexts, id_rows, next_rows = [], [], [], []
    for k in range(2):
        chosen = jnp.logical_and(mine, rank == float(k))
        count = jnp.sum(jnp.where(chosen, 1.0, 0.0), axis=1, keepdims=True)
        one = jnp.sum(jnp.where(chosen, number, 0.0), axis=1, keepdims=True)
        two = jnp.sum(jnp.where(chosen, grid_ref[1], 0.0), axis=1, keepdims=True)
        ids.append(jnp.where(count > 0.5, one, -1.0))
        nexts.append(jnp.where(count > 0.5, two, -2.0))
        id_rows.append(to_row(ids[k], eye))
        next_rows.append(to_row(nexts[k], eye))
    for k in range(2):
        for m in range(2):
            at = (slice(k * n, (k + 1) * n), slice(m * n, (m + 1) * n))
            pair_ref[0, at[0], at[1]] = jnp.where(nexts[k] == id_rows[m], 1.0, 0.0)
            pair_ref[1, at[0], at[1]] = jnp.where(ids[k] == next_rows[m], 1.0, 0.0)

    def aim(r):
        value = tgt_ref[:, lanes(r, LANES)]
        top, middle, low = (part.astype(F32) for part in three_parts(-2.0 * value))
        square = value * value
        for h in range(2):
            at = pl.ds(pl.multiple_of(r * panel + h * LANES, LANES), LANES)
            k = 0
            for c in range(3):
                for part in (top, top, middle, top, low, middle):
                    a_ref[k : k + 1, at] = part[2 * c + h : 2 * c + h + 1]
                    k += 1
            a_ref[k : k + 3, at] = jnp.ones((3, LANES), F32)
            total_square = square[h : h + 1] + square[2 + h : 3 + h] + square[4 + h : 5 + h]
            for m, part in enumerate(three_parts(total_square + CORE_SQUARED)):
                a_ref[k + 3 + m : k + 4 + m, at] = part.astype(F32)

    def add_blocks(first, count, panels):
        b_at = pl.multiple_of(first * 32, 32)
        f_at = pl.multiple_of(first * 16, 16)
        b = jnp.concatenate(
            [b_ref[pl.ds(b_at + 32 * j, 32), :].astype(BF16) for j in range(count)], axis=1
        )
        f = jnp.concatenate(
            [f_ref[pl.ds(f_at + 16 * j, 16), :].astype(BF16) for j in range(count)], axis=1
        )
        for r in panels:
            at = lanes(r, panel)
            a = a_ref[:, at].astype(BF16)
            q = lax.dot_general(b, a, (((0,), (0,)), ((), ())), preferred_element_type=F32)
            root = lax.rsqrt(q)
            top, low = two_parts(root * root * root)
            acc_ref[:, at] += jnp.dot(f, top, preferred_element_type=F32) + jnp.dot(
                f, low, preferred_element_type=F32
            )

    def velocity_of(r):
        value = tgt_ref[:, lanes(r, LANES)]
        for h in range(2):
            at = pl.ds(pl.multiple_of(r * panel + h * LANES, LANES), LANES)
            t = [value[2 * c + h : 2 * c + h + 1] for c in range(3)]
            s = [acc_ref[k : k + 1, at] + acc_ref[8 + k : 9 + k, at] for k in range(6)]
            v = [
                scale * (s[1] * t[2] - s[2] * t[1] - s[3]),
                scale * (s[2] * t[0] - s[0] * t[2] - s[4]),
                scale * (s[0] * t[1] - s[1] * t[0] - s[5]),
            ]
            for c in range(3):
                sum_ref[2 * c + h : 2 * c + h + 1, lanes(r, LANES)] = v[c]

    near = n_row // 2
    far = [k for k in range(1, n_row) if k != near]
    others = [lax.rem(me_r + k, n_row) for k in far]
    near_r = lax.rem(me_r + near, n_row)
    acc_ref[...] = jnp.zeros_like(acc_ref)
    sum_ref[...] = jnp.zeros_like(sum_ref)
    a_ref[...] = jnp.zeros_like(a_ref)
    aim(me_r)
    for first in range(0, slots // 2, SMALL):
        add_blocks(first, SMALL, [me_r])
    wait_from(me_r, n_row, lambda r: piece(tgt_ref, r, width), r3, [near])
    aim(near_r)
    for first in range(0, slots // 2, SMALL):
        add_blocks(first, SMALL, [near_r])
    wait_from(me_r, n_row, lambda r: piece(tgt_ref, r, width), r3, far)
    for copy in copies:
        copy.wait_send()
    for r in others:
        aim(r)

    def tile(ref, device):
        return ref.at[pl.ds(pl.multiple_of(device * 8, 8), 8), :]

    def start_block(step):
        to = lax.rem(me + step, n)
        pltpu.make_async_remote_copy(
            src_ref=tile(send_ref, to),
            dst_ref=tile(arrived_ref, me),
            send_sem=send_sem,
            recv_sem=recv_sem,
            device_id=(to // n_col, lax.rem(to, n_col)),
            device_id_type=MESH,
        ).start()

    turns = slots // CHUNK
    each = (n - 1) // turns
    own = pl.ds(pl.multiple_of(me * 8, 8), 8)
    arrived_ref[own, :] = send_ref[own, :]
    for step in range(each * turns + 1, n):
        start_block(step)

    def chunk(turn, carry):
        for j in range(each):
            start_block(turn * each + (j + 1))
        for first in range(0, CHUNK, PART):
            add_blocks(turn * CHUNK + first, PART, others)
        return carry

    lax.fori_loop(0, turns, chunk, 0)

    rest = pl.ds(0, 8 * (n - 1))
    pltpu.make_async_copy(arrived_ref.at[rest], arrived_ref.at[rest], recv_sem).wait()
    pltpu.make_async_copy(send_ref.at[rest], send_ref.at[rest], send_sem).wait()

    y = [
        jnp.concatenate(
            [arrived_ref[pl.ds(2 * c + k, n, stride=8), :] for k in range(2)], axis=0
        )
        for c in range(3)
    ]
    nxt = pick_rows(pair_ref[0].astype(BF16), y)
    prv = pick_rows(pair_ref[1].astype(BF16), y)
    lane = iota((held, LANES), 1)
    arrays = []
    for c in range(3):
        v, nx, pv = y[c], nxt[c], prv[c]
        a1 = jnp.where(lane < LANES - 1, roll(v, -1), roll(nx, -1))
        a2 = jnp.where(lane < LANES - 2, roll(v, -2), roll(nx, -2))
        b1 = jnp.where(lane < 1, roll(pv, 1), roll(v, 1))
        b2 = jnp.where(lane < 2, roll(pv, 2), roll(v, 2))
        sm = (6.0 * v + 4.0 * (a1 + b1) + (a2 + b2)) * 0.0625
        for k in range(2):
            held_ref[c, pl.ds(k, n, stride=2), :] = sm[k * n : (k + 1) * n]
        after = (
            6.0 * roll(nx, -1) + 4.0 * (roll(nx, -2) + v) + (roll(nx, -3) + roll(v, 1))
        ) * 0.0625
        ahead = jnp.where(lane < LANES - 1, roll(sm, -1), after)
        arrays += [0.5 * (ahead + sm), ahead - sm]
    got = pick_lanes(EDGE_LANES, arrays)
    written = pltpu.make_async_copy(held_ref, smooth_ref, out_sem)
    written.start()
    rows, highs, lows = features(got[0::2], got[1::2])
    for k in range(2):
        at = slice(k * n, (k + 1) * n)
        for m, row in enumerate(rows):
            b_ref[pl.ds((slots + k) * 32 + m, 8, stride=64), :] = row[:, at]
        for m in range(6):
            f_ref[pl.ds((slots + k) * 16 + m, 8, stride=32), :] = highs[m][:, at]
            f_ref[pl.ds((slots + k) * 16 + 8 + m, 8, stride=32), :] = lows[m][:, at]
    add_blocks(slots, 2 * len(EDGE_LANES), others)

    for r in others:
        velocity_of(r)
    for_row = (lambda to: piece(sum_ref, to, LANES), lambda r: row_sum.at[r], s4, r4)
    copies = send_row(*for_row, far)
    for first in range(slots // 2, slots, SMALL):
        add_blocks(first, SMALL, [near_r])
    add_blocks(slots, 2 * len(EDGE_LANES), [near_r])
    velocity_of(near_r)
    copies += send_row(*for_row, [near])
    for first in range(slots // 2, slots, SMALL):
        add_blocks(first, SMALL, [me_r])
    add_blocks(slots, 2 * len(EDGE_LANES), [me_r])
    velocity_of(me_r)
    row_sum[me_r] = sum_ref[:, pl.ds(pl.multiple_of(me_r * LANES, LANES), LANES)]
    wait_from(me_r, n_row, lambda r: row_sum.at[r], r4)
    value = add_up(row_sum, n_row)
    row_total[...] = value
    copies += send_col(row_total, lambda c: col_sum.at[c], s5, r5)
    col_sum[me_c] = value
    wait_from(me_c, n_col, lambda c: col_sum.at[c], r5)
    value = add_up(col_sum, n_col)
    share = vel_ref.shape[2]
    per_row = LANES // share
    first = lax.rem(me_c, per_row) * share
    pick = (iota((LANES, share), 0) == first + iota((LANES, share), 1)).astype(BF16)
    got = [jnp.dot(part, pick, preferred_element_type=F32) for part in three_parts(value)]
    got = got[0] + got[1] + got[2]
    lower = (iota((1, share), 1) + me_c) < iota((1, share), 1) + per_row
    for c in range(3):
        vel_ref[c] = jnp.where(lower, got[2 * c : 2 * c + 1], got[2 * c + 1 : 2 * c + 2])
    for copy in copies:
        copy.wait_send()
    written.wait()


def shards(n_row, n_col, positions, block_links, panel_points):
    devices = n_row * n_col
    slots, block_len = positions.shape[1:]
    held = 2 * devices
    blocks = block_links.shape[1]
    groups, panel = panel_points.shape
    targets = groups * panel
    width = LANES
    stored = slots + 2 * 8
    scale = 1.0 / (math.pi * math.sqrt(blocks * block_len))
    whole = pl.BlockSpec(memory_space=pltpu.VMEM)
    dma = pltpu.SemaphoreType.DMA
    smoothed, velocity = pl.pallas_call(
        functools.partial(step_kernel, n_row, n_col, scale),
        out_shape=(
            jax.ShapeDtypeStruct((3, held, block_len), F32),
            jax.ShapeDtypeStruct((3, 1, panel // n_col), F32),
        ),
        in_specs=[whole, whole, whole],
        out_specs=(pl.BlockSpec(memory_space=pl.ANY), whole),
        scratch_shapes=[
            pltpu.VMEM((2, devices, slots), F32),
            pltpu.VMEM((8, groups * LANES), F32),
            pltpu.VMEM((8, groups * LANES), F32),
            pltpu.VMEM((8 * devices, block_len), F32),
            pltpu.VMEM((8 * devices, block_len), F32),
            pltpu.VMEM((stored * 32, LANES), F32),
            pltpu.VMEM((stored * 16, LANES), F32),
            pltpu.VMEM((32, targets), F32),
            pltpu.VMEM((16, targets), F32),
            pltpu.VMEM((2, held, held), F32),
            pltpu.VMEM((8, groups * LANES), F32),
            pltpu.VMEM((n_row, 8, width), F32),
            pltpu.VMEM((8, width), F32),
            pltpu.VMEM((n_col, 8, width), F32),
            pltpu.VMEM((n_row, 8, LANES), F32),
            pltpu.VMEM((8, LANES), F32),
            pltpu.VMEM((n_col, 8, LANES), F32),
            pltpu.VMEM((3, held, block_len), F32),
            dma, dma, dma,
            dma((n_row,)), dma((n_row,)),
            dma((n_col,)), dma((n_col,)),
            dma((n_row,)), dma((n_row,)),
            dma((n_row,)), dma((n_row,)),
            dma((n_col,)), dma((n_col,)),
        ],
        compiler_params=pltpu.CompilerParams(
            vmem_limit_bytes=VMEM_LIMIT, collective_id=0, has_side_effects=True
        ),
        name="step",
    )(positions, block_links, panel_points)
    return smoothed, jnp.transpose(velocity, (1, 0, 2))


def solution(mesh):
    placed = (P(None, ("row", "col"), None), P(), P())
    return jax.shard_map(
        functools.partial(shards, mesh.shape["row"], mesh.shape["col"]),
        mesh=mesh,
        in_specs=placed,
        out_specs=(P(None, ("row", "col"), None), P("row", None, "col")),
        check_vma=False,
    )
```
